512 devices in a mesh: section: 16 (over x, y), dp: 32 (over z, core).
Axes of the slice: x: 4, y: 4, z: 16, core: 2. Of those that a mesh axis runs over, the one named last changes fastest.
Arguments:
- stream_in: bfloat16 [2, 2048, 3584], P(None, 'dp'), may hold values from -6 to 6
- cotangent: bfloat16 [2, 2048, 3584], P(None, 'dp'), may hold values from -6 to 6
- norm_gain: bfloat16 [16, 3584], P('section'), may hold values from 0.1 to 3.5
- weight_in: bfloat16 [16, 3584, 128], P('section', 'dp'), may hold values from -0.09375 to 0.09375
- weight_out: bfloat16 [16, 128, 3584], P('section', 'dp'), may hold values from -0.5 to 0.5
- moment_in: float32 [16, 3584, 128], P('section', 'dp'), may hold values from -3 to 3
- variance_in: float32 [16, 3584, 128], P('section', 'dp'), may hold values from 0.05 to 2
- moment_out: float32 [16, 128, 3584], P('section', 'dp'), may hold values from -3 to 3
- variance_out: float32 [16, 128, 3584], P('section', 'dp'), may hold values from 0.05 to 2
Outputs:
- weight_in_next: float32 [16, 3584, 128], P('section', 'dp')
- moment_in_next: float32 [16, 3584, 128], P('section', 'dp')
- variance_in_next: float32 [16, 3584, 128], P('section', 'dp')
- weight_out_next: float32 [16, 128, 3584], P('section', 'dp')
- moment_out_next: float32 [16, 128, 3584], P('section', 'dp')
- variance_out_next: float32 [16, 128, 3584], P('section', 'dp')
The draws below stay inside these ranges and needn't reach their ends.
All inputs are finite; a program needn't handle non-finite values.
Results may differ from the reference program's by a relative error of at most 0.02.
Values may be sent and summed in bfloat16 or wider, within the bound.
No kernel may reach another device: no remote copies, remote signals or barrier semaphores. Data moves between devices by JAX's collectives and lax.ppermute only.
A program may use at most 64 MiB of HBM per device.

```python
import math
import jax
import jax.numpy as jnp
from jax import lax

E = 3584
R = 128
MICRO = 2
TOK_DEV = 64
SECTIONS = 16
TOKENS = 2048
N_DP = 32


def draw_norm_gain(key, part):
    section_ramp = 0.5 + jnp.arange(SECTIONS, dtype=jnp.float32)[:, None] / max(SECTIONS - 1, 1)
    channel_ramp = 0.5 + jnp.arange(E, dtype=jnp.float32)[None, :] / E
    jitter = jax.random.uniform(key, (SECTIONS, E), jnp.float32, 0.7, 1.3)
    return (section_ramp * channel_ramp * jitter).astype(jnp.bfloat16)


def raised(drawn, rng, source, target, parts, factor):
    owner, partner = [(jnp.arange(drawn.shape[axis_at]) // (drawn.shape[axis_at] // parts)).reshape([-1 if axis == axis_at else 1 for axis in range(drawn.ndim)]) for axis_at in (source, target)]
    chosen = jax.random.permutation(rng, parts)[partner]
    strong = (owner == chosen) | (owner == (partner + parts // 2) % parts)
    return jnp.where(strong, factor * drawn, drawn)


def block_scale(rng, shape, cuts, low, largest):
    loudness = 1.0
    for axis_at, parts in cuts:
        heights = jax.random.uniform(jax.random.fold_in(jax.random.fold_in(rng, 6), axis_at), (parts,), jnp.float32, low / len(cuts), largest / len(cuts))
        loudness = loudness * jnp.repeat(jnp.exp(heights), shape[axis_at] // parts).reshape((-1,) + (1,) * (len(shape) - 1 - axis_at))
    return loudness


def centred(rng, shape, deviation, reach, split=(), kind=jnp.bfloat16):
    entries = deviation * jax.random.normal(rng, shape, jnp.float32)
    if split:
        entries = entries * block_scale(rng, shape, split, -0.22, 0.18)
    return jnp.clip(entries, -reach, reach).astype(kind)


def bell_draw_with(rng, dims, scale, limit, split, heavy, held_as=jnp.bfloat16):
    array = scale * jax.random.normal(rng, dims, jnp.float32)
    if split:
        array = array * block_scale(rng, dims, split, -0.22, 0.18)
    return jnp.clip(raised(array, jax.random.fold_in(rng, 3), *heavy), -limit, limit).astype(held_as)


def setup_inputs(seed: int = 0) -> dict:
    seeds = jax.random.split(jax.random.key(seed), 10)
    stream_in = bell_draw_with(seeds[0], (MICRO, TOKENS, E), 1.0, 6.0, ((1, 32),), (1, 2, 32, 2.75))
    cotangent = centred(seeds[1], (MICRO, TOKENS, E), 1.0, 6.0, ((1, 32),))
    norm_gain = draw_norm_gain(jax.random.fold_in(seeds[9], 71), 0)
    weight_in = centred(seeds[3], (SECTIONS, E, R), E ** -0.5, 0.09375, ((0, 16), (1, 32)))
    weight_out = centred(seeds[4], (SECTIONS, R, E), R ** -0.5, 0.5, ((0, 16), (1, 32)))
    moment_in = centred(seeds[5], (SECTIONS, E, R), 0.5, 3.0, ((0, 16), (1, 32)), jnp.float32)
    variance_in = jnp.clip(jnp.exp(math.log(2.0) - 3.6888794 * jax.random.uniform(seeds[6], (SECTIONS, E, R), jnp.float32) ** block_scale(seeds[6], (SECTIONS, E, R), ((0, 16), (1, 32)), -0.2, 0.2)), 0.05, 2.0)
    moment_out = centred(seeds[7], (SECTIONS, R, E), 0.5, 3.0, ((0, 16), (1, 32)), jnp.float32)
    variance_out = jnp.clip(jnp.exp(math.log(2.0) - 3.6888794 * jax.random.uniform(seeds[8], (SECTIONS, R, E), jnp.float32) ** block_scale(seeds[8], (SECTIONS, R, E), ((0, 16), (1, 32)), -0.2, 0.2)), 0.05, 2.0)
    return {"stream_in": stream_in, "cotangent": cotangent, "norm_gain": norm_gain, "weight_in": weight_in, "weight_out": weight_out, "moment_in": moment_in, "variance_in": variance_in, "moment_out": moment_out, "variance_out": variance_out}


NORM_EPS = 1e-06
BETA_ONE = 0.9
BETA_TWO = 0.95
STEP_RATE = 0.01
ADAM_EPS = 1e-08
CLIP_EPS = 1e-06

def normalize(stream, gain):
    values = stream.astype(jnp.float32)
    inv_root = lax.rsqrt(lax.optimization_barrier(jnp.mean(values * values, axis=-1, keepdims=True)) + NORM_EPS)
    unit_rows = values * inv_root
    normed = (unit_rows * gain.astype(jnp.float32)).astype(jnp.bfloat16)
    return (values, inv_root, unit_rows, normed)

def section_forward(stream, gain, in_weight, out_weight):
    values, inv_root, unit_rows, normed = normalize(stream, gain)
    pre_act = jnp.dot(normed, in_weight, preferred_element_type=jnp.float32)
    hidden = (pre_act * jax.nn.sigmoid(pre_act)).astype(jnp.bfloat16)
    return (values + jnp.dot(hidden, out_weight, preferred_element_type=jnp.float32)).astype(jnp.bfloat16)

def section_backward(stream, grad_rows, gain, in_weight, out_weight):
    values, inv_root, unit_rows, normed = normalize(stream, gain)
    pre_act = jnp.dot(normed, in_weight, preferred_element_type=jnp.float32)
    squash = jax.nn.sigmoid(pre_act)
    hidden = (pre_act * squash).astype(jnp.bfloat16)
    grad_hidden = lax.dot_general(grad_rows, out_weight, (((1,), (1,)), ((), ())), preferred_element_type=jnp.float32)
    grad_act = (grad_hidden * squash * (1.0 + pre_act * (1.0 - squash))).astype(jnp.bfloat16)
    grad_normed = lax.dot_general(grad_act, in_weight, (((1,), (1,)), ((), ())), preferred_element_type=jnp.float32) * gain.astype(jnp.float32)
    inner_mean = lax.optimization_barrier(jnp.mean(grad_normed * unit_rows, axis=-1, keepdims=True))
    grad_in = (grad_rows.astype(jnp.float32) + inv_root * (grad_normed - unit_rows * inner_mean)).astype(jnp.bfloat16)
    return (grad_in, normed, grad_act, hidden)

def grouped(left, right):
    left_width = left.shape[-1]
    right_width = right.shape[-1]
    left = left.reshape(2, MICRO // 2, N_DP, TOK_DEV, left_width).transpose(0, 2, 1, 3, 4)
    left = left.reshape(2 * N_DP, MICRO // 2 * TOK_DEV, left_width)
    right = right.reshape(2, MICRO // 2, N_DP, TOK_DEV, right_width).transpose(0, 2, 1, 3, 4)
    right = right.reshape(2 * N_DP, MICRO // 2 * TOK_DEV, right_width)

    def add_part(running, pair):
        part = lax.dot_general(pair[0], pair[1], (((0,), (0,)), ((), ())), preferred_element_type=jnp.float32)
        rounded = lax.optimization_barrier(part.astype(jnp.bfloat16))
        return (running + rounded.astype(jnp.float32), None)
    running, _ = lax.scan(add_part, jnp.zeros((left_width, right_width), jnp.float32), (left, right))
    return running

def update(weight, grad, moment, variance, factor):
    scaled = factor * grad
    moment = BETA_ONE * moment + (1.0 - BETA_ONE) * scaled
    variance = BETA_TWO * variance + (1.0 - BETA_TWO) * scaled * scaled
    weight = weight.astype(jnp.float32) - STEP_RATE * moment / (jnp.sqrt(variance) + ADAM_EPS)
    return (weight, moment, variance)

def reference(stream_in, cotangent, norm_gain, weight_in, weight_out, moment_in, variance_in, moment_out, variance_out):
    all_rows = stream_in.reshape(-1, E)
    all_grads = cotangent.reshape(-1, E)

    def forward(stream, layer_params):
        gain, in_weight, out_weight = layer_params
        return (section_forward(stream, gain, in_weight, out_weight), stream)
    _, saved_rows = lax.scan(forward, all_rows, (norm_gain, weight_in, weight_out))

    def backward(grad_rows, layer_params):
        stream, gain, in_weight, out_weight = layer_params
        grad_in, normed, grad_act, hidden = section_backward(stream, grad_rows, gain, in_weight, out_weight)
        return (grad_in, (grouped(normed, grad_act), grouped(hidden, grad_rows)))
    _, (grad_w_in, grad_w_out) = lax.scan(backward, all_grads, (saved_rows, norm_gain, weight_in, weight_out), reverse=True)
    norm_total = jnp.sum(grad_w_in * grad_w_in) + jnp.sum(grad_w_out * grad_w_out)
    count_all = 2.0 * SECTIONS * E * R
    factor = jnp.minimum(1.0, lax.rsqrt(norm_total / count_all + CLIP_EPS))
    new_in, new_moment_in, new_variance_in = update(weight_in, grad_w_in, moment_in, variance_in, factor)
    new_out, new_moment_out, new_variance_out = update(weight_out, grad_w_out, moment_out, variance_out, factor)
    return (new_in, new_moment_in, new_variance_in, new_out, new_moment_out, new_variance_out)
```

```python
import jax
import jax.numpy as jnp
from jax import lax
from jax.experimental import pallas as pl
from jax.experimental.pallas import tpu as pltpu
from jax.sharding import Mesh
from jax.sharding import PartitionSpec as P

E = 3584
R = 128
SECTIONS = 16
ROWS = 128
STEP = 256
LANES = 128
COLS = E // LANES
RINGS = 16
SECTION = ("section_0", "section_1")
DP = ("dp_0", "dp_1")
SECTION_DP = ("section_0", "section_1", "dp_0", "dp_1")

NORM_EPS = 1e-06
BETA_ONE = 0.9
BETA_TWO = 0.95
STEP_RATE = 0.01
ADAM_EPS = 1e-08
CLIP_EPS = 1e-06


def nt_dot(left, right):
    return lax.dot_general(
        left, right, (((1,), (1,)), ((), ())), preferred_element_type=jnp.float32
    )


def tn_dot(left, right):
    return lax.dot_general(
        left, right, (((0,), (0,)), ((), ())), preferred_element_type=jnp.float32
    )


def chain(
    place, stream, target, flat, tiles, grad_in, grad_out, w_in, w_out, kept, grad, pre, root,
    hid, staged, sems, out_sems
):
    def loads(k):
        copies = [pltpu.make_async_copy(flat.at[k, 0], w_in.at[k], sems.at[k, 0])]
        for z in range(RINGS):
            copies.append(
                pltpu.make_async_copy(
                    tiles.at[k, 1, z], w_out.at[k, :, pl.ds(z * 8, 8), :], sems.at[k, 1 + z]
                )
            )
        return copies

    def start(k, _):
        for c in loads(k):
            c.start()
        return 0

    def wait(k):
        for c in loads(k):
            c.wait()

    lax.fori_loop(0, SECTIONS, start, 0)
    kept[0] = stream[...]

    def out_part(k, c):
        return jnp.concatenate([w_out[k, 2 * c], w_out[k, 2 * c + 1]], axis=1)

    def squares(values):
        return values[:, :LANES] * values[:, :LANES] + values[:, LANES:] * values[:, LANES:]

    def finish(k, acc, total):
        mean = jnp.sum(total, axis=1, keepdims=True) * (1.0 / E)
        inv = lax.rsqrt(mean + NORM_EPS)
        pre[k] = acc * inv
        root[k] = jnp.broadcast_to(inv, (ROWS, LANES))

    wait(0)
    acc = jnp.zeros((ROWS, R), jnp.float32)
    total = jnp.zeros((ROWS, LANES), jnp.float32)
    for c in range(E // STEP):
        rows = stream[:, c * STEP : (c + 1) * STEP]
        total += squares(rows.astype(jnp.float32))
        acc += jnp.dot(
            rows, w_in[0, c * STEP : (c + 1) * STEP], preferred_element_type=jnp.float32
        )
    finish(0, acc, total)

    def forward(k, _):
        wait(k + 1)
        p = pre[k]
        hidden = (p * jax.nn.sigmoid(p)).astype(jnp.bfloat16)
        acc = jnp.zeros((ROWS, R), jnp.float32)
        total = jnp.zeros((ROWS, LANES), jnp.float32)
        for c in range(E // STEP):
            at = slice(c * STEP, (c + 1) * STEP)
            rows = kept[k, :, at].astype(jnp.float32) + jnp.dot(
                hidden, out_part(k, c), preferred_element_type=jnp.float32
            )
            rows = rows.astype(jnp.bfloat16)
            kept[k + 1, :, at] = rows
            total += squares(rows.astype(jnp.float32))
            acc += jnp.dot(rows, w_in[k + 1, at], preferred_element_type=jnp.float32)
        finish(k + 1, acc, total)
        return 0

    lax.fori_loop(0, SECTIONS - 1, forward, 0)

    acc = jnp.zeros((ROWS, R), jnp.float32)
    for c in range(E // STEP):
        at = slice(c * STEP, (c + 1) * STEP)
        rows = target[:, at]
        grad[:, at] = rows
        acc += nt_dot(rows, out_part(SECTIONS - 1, c))
    hid[...] = acc

    def backward(i, _):
        k = SECTIONS - 1 - i
        p = pre[k]
        inv = root[k]
        squash = jax.nn.sigmoid(p)
        act = hid[...] * squash * (1.0 + p * (1.0 - squash))
        inner = jnp.sum(act * p, axis=1, keepdims=True) * (1.0 / E)
        scaled = (inv * act).astype(jnp.bfloat16)
        back = inv * inv * inner
        wide = jnp.concatenate([back, back], axis=1)

        @pl.when(k == place[0])
        def _():
            hidden = (p * squash).astype(jnp.bfloat16)
            for c in range(E // STEP):
                at = slice(c * STEP, (c + 1) * STEP)
                part = tn_dot(hidden, grad[:, at]).astype(jnp.bfloat16)
                staged[2 * c] = part[:, :LANES]
                staged[2 * c + 1] = part[:, LANES:]
                grad_in[at] = tn_dot(kept[k, :, at], scaled).astype(jnp.bfloat16)

        @pl.when(k > 0)
        def _():
            acc = jnp.zeros((ROWS, R), jnp.float32)
            for c in range(E // STEP):
                at = slice(c * STEP, (c + 1) * STEP)
                rows = grad[:, at].astype(jnp.float32) + nt_dot(scaled, w_in[k, at])
                rows = (rows - wide * kept[k, :, at].astype(jnp.float32)).astype(jnp.bfloat16)
                grad[:, at] = rows
                acc += nt_dot(rows, out_part(k - 1, c))
            hid[...] = acc

        return 0

    lax.fori_loop(0, SECTIONS, backward, 0)
    stores = [
        pltpu.make_async_copy(staged.at[:, pl.ds(z * 8, 8), :], grad_out.at[z], out_sems.at[z])
        for z in range(RINGS)
    ]
    for c in stores:
        c.start()
    for c in stores:
        c.wait()


def run_chain(place, stream, target, gathered):
    flat = gathered.reshape(SECTIONS, 2, E, R)
    tiles = gathered.reshape(SECTIONS, 2, RINGS, COLS, 8, LANES)
    whole = pl.BlockSpec(memory_space=pltpu.VMEM)
    anywhere = pl.BlockSpec(memory_space=pl.ANY)
    return pl.pallas_call(
        chain,
        out_shape=(
            jax.ShapeDtypeStruct((E, R), jnp.bfloat16),
            jax.ShapeDtypeStruct((RINGS, COLS, 8, LANES), jnp.bfloat16),
        ),
        in_specs=[pl.BlockSpec(memory_space=pltpu.SMEM), whole, whole, anywhere, anywhere],
        out_specs=(whole, anywhere),
        scratch_shapes=[
            pltpu.VMEM((SECTIONS, E, R), jnp.bfloat16),
            pltpu.VMEM((SECTIONS, COLS, R, LANES), jnp.bfloat16),
            pltpu.VMEM((SECTIONS, ROWS, E), jnp.bfloat16),
            pltpu.VMEM((ROWS, E), jnp.bfloat16),
            pltpu.VMEM((SECTIONS, ROWS, R), jnp.float32),
            pltpu.VMEM((SECTIONS, ROWS, LANES), jnp.float32),
            pltpu.VMEM((ROWS, R), jnp.float32),
            pltpu.VMEM((COLS, R, LANES), jnp.bfloat16),
            pltpu.SemaphoreType.DMA((SECTIONS, 1 + RINGS)),
            pltpu.SemaphoreType.DMA((RINGS,)),
        ],
        compiler_params=pltpu.CompilerParams(vmem_limit_bytes=60 * 1024 * 1024),
    )(place, stream, target, flat, tiles)


def swap_cores(x):
    return lax.ppermute(x, "dp_1", [(0, 1), (1, 0)])


def update(weight, grad, moment, variance, factor):
    scaled = factor * grad
    moment = BETA_ONE * moment + (1.0 - BETA_ONE) * scaled
    variance = BETA_TWO * variance + (1.0 - BETA_TWO) * scaled * scaled
    weight = weight.astype(jnp.float32) - STEP_RATE * moment / (jnp.sqrt(variance) + ADAM_EPS)
    return (weight[None], moment[None], variance[None])


def shards(
    stream_in,
    cotangent,
    norm_gain,
    weight_in,
    weight_out,
    moment_in,
    variance_in,
    moment_out,
    variance_out,
):
    section = lax.axis_index(SECTION)
    ring = lax.axis_index("dp_0")
    core = lax.axis_index("dp_1")
    first = core == 0
    dp = lax.axis_index(DP)
    in_slice = weight_in[0]
    out_slice = weight_out[0]
    own_rows = in_slice.shape[0]
    gain = lax.dynamic_slice_in_dim(norm_gain[0], dp * own_rows, own_rows).astype(jnp.float32)

    in_part = (in_slice.astype(jnp.float32) * gain[:, None]).astype(jnp.bfloat16)
    in_part = in_part.reshape(COLS, 4, LANES)
    out_part = out_slice.reshape(4, COLS, LANES).transpose(1, 0, 2)
    other = swap_cores(jnp.where(first, out_part, in_part))
    of_in = jnp.concatenate([in_part, other], axis=0).reshape(COLS, 8, LANES)
    of_out = jnp.concatenate([other, out_part], axis=1)
    pair = jnp.where(first, of_in, of_out)
    column = lax.all_gather(pair[None], "dp_0", axis=0, tiled=True)
    gathered = lax.all_gather(column, SECTION + ("dp_1",), axis=0, tiled=True)

    place = jnp.stack([section, core]).astype(jnp.int32)
    grad_in, grad_out = run_chain(
        place, stream_in.reshape(ROWS, E), cotangent.reshape(ROWS, E), gathered
    )
    grad_in = grad_in.reshape(RINGS, COLS, 8, LANES)
    keep = jnp.where(first, grad_in, grad_out)
    got = swap_cores(jnp.where(first, grad_out, grad_in))
    both = (keep.astype(jnp.float32) + got.astype(jnp.float32)).astype(jnp.bfloat16)
    pieces = lax.all_to_all(both, "dp_0", 0, 0, tiled=True)
    total = jnp.sum(pieces.astype(jnp.float32), axis=0)
    as_in = total.reshape(2, own_rows, LANES)
    as_out = total.reshape(COLS, 2, 4, LANES)
    mine = jnp.where(first, as_in[0], as_out[:, 1].reshape(own_rows, LANES))
    theirs = jnp.where(first, as_in[1], as_out[:, 0].reshape(own_rows, LANES))
    arrived = swap_cores(theirs)
    grad_w_in = jnp.where(first, mine, arrived) * gain[:, None]
    grad_w_out = jnp.where(first, arrived, mine).reshape(COLS, 4, LANES)
    grad_w_out = grad_w_out.transpose(1, 0, 2).reshape(4, E)

    local_sum = jnp.sum(grad_w_in * grad_w_in) + jnp.sum(grad_w_out * grad_w_out)
    norm_total = local_sum
    for axis in SECTION_DP:
        norm_total = lax.psum(norm_total, axis)
    count_all = 2.0 * E * R * SECTIONS
    factor = jnp.minimum(1.0, lax.rsqrt(norm_total / count_all + CLIP_EPS))
    new_in, new_moment_in, new_variance_in = update(
        in_slice, grad_w_in, moment_in[0], variance_in[0], factor
    )
    new_out, new_moment_out, new_variance_out = update(
        out_slice, grad_w_out, moment_out[0], variance_out[0], factor
    )
    return (new_in, new_moment_in, new_variance_in, new_out, new_moment_out, new_variance_out)


def solution(mesh):
    finer = Mesh(mesh.devices.reshape(4, 4, 16, 2), SECTION_DP)
    placed = (P(None, DP, None), P(None, DP, None), P(SECTION, None)) + 6 * (
        P(SECTION, DP, None),
    )
    return jax.shard_map(
        shards, mesh=finer, in_specs=placed, out_specs=6 * (P(SECTION, DP, None),), check_vma=False
    )
```

```python
import jax
import jax.numpy as jnp
from jax import lax
from jax.experimental import pallas as pl
from jax.experimental.pallas import tpu as pltpu
from jax.sharding import Mesh
from jax.sharding import PartitionSpec as P

E = 3584
R = 128
SECTIONS = 16
ROWS = 128
STEP = 256
LANES = 128
COLS = E // LANES
RINGS = 16
SECTION = ("section_0", "section_1")
RING = ("ring_0", "ring_1")
DP = RING + ("dp_1",)
EVERY = SECTION + DP

NORM_EPS = 1e-06
BETA_ONE = 0.9
BETA_TWO = 0.95
STEP_RATE = 0.01
ADAM_EPS = 1e-08
CLIP_EPS = 1e-06


def nt_dot(left, right):
    return lax.dot_general(
        left, right, (((1,), (1,)), ((), ())), preferred_element_type=jnp.float32
    )


def tn_dot(left, right):
    return lax.dot_general(
        left, right, (((0,), (0,)), ((), ())), preferred_element_type=jnp.float32
    )


def chain(
    place, stream, target, flat, tiles, grad_in, grad_out, w_in, w_out, kept, grad, pre, root,
    hid, staged, sems, out_sems
):
    def loads(k):
        copies = [pltpu.make_async_copy(flat.at[k, 0], w_in.at[k], sems.at[k, 0])]
        for z in range(RINGS):
            copies.append(
                pltpu.make_async_copy(
                    tiles.at[k, 1, z], w_out.at[k, :, pl.ds(z * 8, 8), :], sems.at[k, 1 + z]
                )
            )
        return copies

    def start(k, _):
        for c in loads(k):
            c.start()
        return 0

    def wait(k):
        for c in loads(k):
            c.wait()

    lax.fori_loop(0, SECTIONS, start, 0)
    kept[0] = stream[...]

    def out_part(k, c):
        return jnp.concatenate([w_out[k, 2 * c], w_out[k, 2 * c + 1]], axis=1)

    def squares(values):
        return values[:, :LANES] * values[:, :LANES] + values[:, LANES:] * values[:, LANES:]

    def finish(k, acc, total):
        mean = jnp.sum(total, axis=1, keepdims=True) * (1.0 / E)
        inv = lax.rsqrt(mean + NORM_EPS)
        pre[k] = acc * inv
        root[k] = jnp.broadcast_to(inv, (ROWS, LANES))

    wait(0)
    acc = jnp.zeros((ROWS, R), jnp.float32)
    total = jnp.zeros((ROWS, LANES), jnp.float32)
    for c in range(E // STEP):
        rows = stream[:, c * STEP : (c + 1) * STEP]
        total += squares(rows.astype(jnp.float32))
        acc += jnp.dot(
            rows, w_in[0, c * STEP : (c + 1) * STEP], preferred_element_type=jnp.float32
        )
    finish(0, acc, total)

    def forward(k, _):
        wait(k + 1)
        p = pre[k]
        hidden = (p * jax.nn.sigmoid(p)).astype(jnp.bfloat16)
        acc = jnp.zeros((ROWS, R), jnp.float32)
        total = jnp.zeros((ROWS, LANES), jnp.float32)
        for c in range(E // STEP):
            at = slice(c * STEP, (c + 1) * STEP)
            rows = kept[k, :, at].astype(jnp.float32) + jnp.dot(
                hidden, out_part(k, c), preferred_element_type=jnp.float32
            )
            rows = rows.astype(jnp.bfloat16)
            kept[k + 1, :, at] = rows
            total += squares(rows.astype(jnp.float32))
            acc += jnp.dot(rows, w_in[k + 1, at], preferred_element_type=jnp.float32)
        finish(k + 1, acc, total)
        return 0

    lax.fori_loop(0, SECTIONS - 1, forward, 0)

    acc = jnp.zeros((ROWS, R), jnp.float32)
    for c in range(E // STEP):
        at = slice(c * STEP, (c + 1) * STEP)
        rows = target[:, at]
        grad[:, at] = rows
        acc += nt_dot(rows, out_part(SECTIONS - 1, c))
    hid[...] = acc

    def backward(i, _):
        k = SECTIONS - 1 - i
        p = pre[k]
        inv = root[k]
        squash = jax.nn.sigmoid(p)
        act = hid[...] * squash * (1.0 + p * (1.0 - squash))
        inner = jnp.sum(act * p, axis=1, keepdims=True) * (1.0 / E)
        scaled = (inv * act).astype(jnp.bfloat16)
        back = inv * inv * inner
        wide = jnp.concatenate([back, back], axis=1)

        @pl.when(k == place[0])
        def _():
            hidden = (p * squash).astype(jnp.bfloat16)
            for c in range(E // STEP):
                at = slice(c * STEP, (c + 1) * STEP)
                part = tn_dot(hidden, grad[:, at]).astype(jnp.bfloat16)
                staged[2 * c] = part[:, :LANES]
                staged[2 * c + 1] = part[:, LANES:]
                grad_in[at] = tn_dot(kept[k, :, at], scaled).astype(jnp.bfloat16)

        @pl.when(k > 0)
        def _():
            acc = jnp.zeros((ROWS, R), jnp.float32)
            for c in range(E // STEP):
                at = slice(c * STEP, (c + 1) * STEP)
                rows = grad[:, at].astype(jnp.float32) + nt_dot(scaled, w_in[k, at])
                rows = (rows - wide * kept[k, :, at].astype(jnp.float32)).astype(jnp.bfloat16)
                grad[:, at] = rows
                acc += nt_dot(rows, out_part(k - 1, c))
            hid[...] = acc

        return 0

    lax.fori_loop(0, SECTIONS, backward, 0)
    stores = [
        pltpu.make_async_copy(staged.at[:, pl.ds(z * 8, 8), :], grad_out.at[z], out_sems.at[z])
        for z in range(RINGS)
    ]
    for c in stores:
        c.start()
    for c in stores:
        c.wait()


def run_chain(place, stream, target, gathered):
    flat = gathered.reshape(SECTIONS, 2, E, R)
    tiles = gathered.reshape(SECTIONS, 2, RINGS, COLS, 8, LANES)
    whole = pl.BlockSpec(memory_space=pltpu.VMEM)
    anywhere = pl.BlockSpec(memory_space=pl.ANY)
    return pl.pallas_call(
        chain,
        out_shape=(
            jax.ShapeDtypeStruct((E, R), jnp.bfloat16),
            jax.ShapeDtypeStruct((RINGS, COLS, 8, LANES), jnp.bfloat16),
        ),
        in_specs=[pl.BlockSpec(memory_space=pltpu.SMEM), whole, whole, anywhere, anywhere],
        out_specs=(whole, anywhere),
        scratch_shapes=[
            pltpu.VMEM((SECTIONS, E, R), jnp.bfloat16),
            pltpu.VMEM((SECTIONS, COLS, R, LANES), jnp.bfloat16),
            pltpu.VMEM((SECTIONS, ROWS, E), jnp.bfloat16),
            pltpu.VMEM((ROWS, E), jnp.bfloat16),
            pltpu.VMEM((SECTIONS, ROWS, R), jnp.float32),
            pltpu.VMEM((SECTIONS, ROWS, LANES), jnp.float32),
            pltpu.VMEM((ROWS, R), jnp.float32),
            pltpu.VMEM((COLS, R, LANES), jnp.bfloat16),
            pltpu.SemaphoreType.DMA((SECTIONS, 1 + RINGS)),
            pltpu.SemaphoreType.DMA((RINGS,)),
        ],
        compiler_params=pltpu.CompilerParams(vmem_limit_bytes=60 * 1024 * 1024),
    )(place, stream, target, flat, tiles)


def swap_cores(x):
    return lax.ppermute(x, "dp_1", [(0, 1), (1, 0)])


def update(weight, grad, moment, variance, factor):
    scaled = factor * grad
    moment = BETA_ONE * moment + (1.0 - BETA_ONE) * scaled
    variance = BETA_TWO * variance + (1.0 - BETA_TWO) * scaled * scaled
    weight = weight.astype(jnp.float32) - STEP_RATE * moment / (jnp.sqrt(variance) + ADAM_EPS)
    return (weight[None], moment[None], variance[None])


def shards(
    stream_in,
    cotangent,
    norm_gain,
    weight_in,
    weight_out,
    moment_in,
    variance_in,
    moment_out,
    variance_out,
):
    section = lax.axis_index(SECTION)
    ring = lax.axis_index(RING)
    core = lax.axis_index("dp_1")
    first = core == 0
    dp = lax.axis_index(DP)
    in_slice = weight_in[0]
    out_slice = weight_out[0]
    own_rows = in_slice.shape[0]
    gain = lax.dynamic_slice_in_dim(norm_gain[0], dp * own_rows, own_rows).astype(jnp.float32)

    in_part = (in_slice.astype(jnp.float32) * gain[:, None]).astype(jnp.bfloat16)
    in_part = in_part.reshape(COLS, 4, LANES)
    out_part = out_slice.reshape(4, COLS, LANES).transpose(1, 0, 2)
    other = swap_cores(jnp.where(first, out_part, in_part))
    of_in = jnp.concatenate([in_part, other], axis=0).reshape(COLS, 8, LANES)
    of_out = jnp.concatenate([other, out_part], axis=1)
    pair = jnp.where(first, of_in, of_out)
    column = lax.all_gather(pair[None], RING, axis=0, tiled=True)
    gathered = lax.all_gather(column, SECTION + ("dp_1",), axis=0, tiled=True)

    place = jnp.stack([section, core]).astype(jnp.int32)
    grad_in, grad_out = run_chain(
        place, stream_in.reshape(ROWS, E), cotangent.reshape(ROWS, E), gathered
    )
    grad_in = grad_in.reshape(RINGS, COLS, 8, LANES)
    keep = jnp.where(first, grad_in, grad_out)
    got = swap_cores(jnp.where(first, grad_out, grad_in))
    total = keep.astype(jnp.float32) + got.astype(jnp.float32)
    total = jnp.swapaxes(total.reshape(4, 4, COLS, 8, LANES), 0, 1)
    for axis in ("ring_1", "ring_0"):
        pieces = lax.all_to_all(total.astype(jnp.bfloat16), axis, 0, 0, tiled=True)
        total = jnp.sum(pieces.astype(jnp.float32), axis=0)
    chip_gain = lax.dynamic_slice_in_dim(norm_gain[0], ring * 2 * own_rows, 2 * own_rows)
    total = total.reshape(2 * own_rows, LANES)
    total = total * jnp.where(first, chip_gain.astype(jnp.float32), 1.0)[:, None]
    chip_sum = jnp.sum(total * total)
    device_count = lax.axis_size(EVERY)
    sums = jnp.broadcast_to(chip_sum, (device_count, 1, LANES))
    sums = lax.all_to_all(sums, EVERY, 0, 0, tiled=True)
    norm_total = jnp.sum(sums[:, 0, 0])

    as_in = total.reshape(2, own_rows, LANES)
    as_out = total.reshape(COLS, 2, 4, LANES)
    mine = jnp.where(first, as_in[0], as_out[:, 1].reshape(own_rows, LANES))
    theirs = jnp.where(first, as_in[1], as_out[:, 0].reshape(own_rows, LANES))
    arrived = swap_cores(theirs)
    grad_w_in = jnp.where(first, mine, arrived)
    grad_w_out = jnp.where(first, arrived, mine).reshape(COLS, 4, LANES)
    grad_w_out = grad_w_out.transpose(1, 0, 2).reshape(4, E)

    count_all = 2.0 * E * R * SECTIONS
    factor = jnp.minimum(1.0, lax.rsqrt(norm_total / count_all + CLIP_EPS))
    new_in, new_moment_in, new_variance_in = update(
        in_slice, grad_w_in, moment_in[0], variance_in[0], factor
    )
    new_out, new_moment_out, new_variance_out = update(
        out_slice, grad_w_out, moment_out[0], variance_out[0], factor
    )
    return (new_in, new_moment_in, new_variance_in, new_out, new_moment_out, new_variance_out)


def solution(mesh):
    finer = Mesh(mesh.devices.reshape(4, 4, 4, 4, 2), EVERY)
    placed = (P(None, DP, None), P(None, DP, None), P(SECTION, None)) + 6 * (
        P(SECTION, DP, None),
    )
    return jax.shard_map(
        shards, mesh=finer, in_specs=placed, out_specs=6 * (P(SECTION, DP, None),), check_vma=False
    )
```

```python
import jax
import jax.numpy as jnp
from jax import lax
from jax.experimental import pallas as pl
from jax.experimental.pallas import tpu as pltpu
from jax.sharding import Mesh
from jax.sharding import PartitionSpec as P

E = 3584
R = 128
SECTIONS = 16
ROWS = 128
STEP = 256
LANES = 128
COLS = E // LANES
RINGS = 16
TILE_ROWS = E // 32
SECTION = ("section_0", "section_1")
RING = ("ring_0", "ring_1")
DP = RING + ("dp_1",)
EVERY = SECTION + DP

NORM_EPS = 1e-06
BETA_ONE = 0.9
BETA_TWO = 0.95
STEP_RATE = 0.01
ADAM_EPS = 1e-08
CLIP_EPS = 1e-06


def nt_dot(left, right):
    return lax.dot_general(
        left, right, (((1,), (1,)), ((), ())), preferred_element_type=jnp.float32
    )


def tn_dot(left, right):
    return lax.dot_general(
        left, right, (((0,), (0,)), ((), ())), preferred_element_type=jnp.float32
    )


def chain(
    place, stream, target, own, own_tiles, rest, rest_tiles, *more
):
    quarters = [more[2 * i : 2 * i + 2] for i in range(4)]
    (
        kept_out, sent_out, w_in, w_out, kept, grad, pre, root, hid, grad_in, staged, sems, out_sems
    ) = more[8:]
    core = place[1]
    own_ring = 4 * place[2]
    far_ring = 4 - own_ring

    def copies(k, sources, at, ring, sem):
        flat, tiles = sources
        rings = tiles.shape[1]
        first_row = pl.multiple_of(ring * 2 * TILE_ROWS, 8)
        out = [
            pltpu.make_async_copy(
                flat.at[at], w_in.at[k, pl.ds(first_row, flat.shape[1]), :], sems.at[k, sem]
            )
        ]
        for z in range(rings):
            row = pl.multiple_of((ring + z) * 8, 8)
            out.append(
                pltpu.make_async_copy(
                    tiles.at[at + 1, z], w_out.at[k, :, pl.ds(row, 8), :], sems.at[k, sem + 1 + z]
                )
            )
        return out

    def loads(k, far, far_at):
        return (
            copies(k, (own, own_tiles), 2 * k, own_ring, 0)
            + copies(k, far, far_at, far_ring, 5)
            + copies(k, (rest, rest_tiles), 2 * k, 8, 10)
        )

    for t in range(4):
        for swapped in range(2):

            @pl.when(core == swapped)
            def _():
                def start(i, _):
                    for c in loads(4 * t + i, quarters[t ^ (2 * swapped)], 2 * i):
                        c.start()
                    return 0

                lax.fori_loop(0, 4, start, 0)

    def wait(k):
        for c in loads(k, quarters[0], 0):
            c.wait()

    kept[0] = stream[...]

    def out_part(k, c):
        return jnp.concatenate([w_out[k, 2 * c], w_out[k, 2 * c + 1]], axis=1)

    def squares(values):
        return values[:, :LANES] * values[:, :LANES] + values[:, LANES:] * values[:, LANES:]

    def finish(k, acc, total):
        mean = jnp.sum(total, axis=1, keepdims=True) * (1.0 / E)
        inv = lax.rsqrt(mean + NORM_EPS)
        pre[k] = acc * inv
        root[k] = jnp.broadcast_to(inv, (ROWS, LANES))

    wait(0)
    acc = jnp.zeros((ROWS, R), jnp.float32)
    total = jnp.zeros((ROWS, LANES), jnp.float32)
    for c in range(E // STEP):
        rows = stream[:, c * STEP : (c + 1) * STEP]
        total += squares(rows.astype(jnp.float32))
        acc += jnp.dot(
            rows, w_in[0, c * STEP : (c + 1) * STEP], preferred_element_type=jnp.float32
        )
    finish(0, acc, total)

    def forward(k, _):
        wait(k + 1)
        p = pre[k]
        hidden = (p * jax.nn.sigmoid(p)).astype(jnp.bfloat16)
        acc = jnp.zeros((ROWS, R), jnp.float32)
        total = jnp.zeros((ROWS, LANES), jnp.float32)
        for c in range(E // STEP):
            at = slice(c * STEP, (c + 1) * STEP)
            rows = kept[k, :, at].astype(jnp.float32) + jnp.dot(
                hidden, out_part(k, c), preferred_element_type=jnp.float32
            )
            rows = rows.astype(jnp.bfloat16)
            kept[k + 1, :, at] = rows
            total += squares(rows.astype(jnp.float32))
            acc += jnp.dot(rows, w_in[k + 1, at], preferred_element_type=jnp.float32)
        finish(k + 1, acc, total)
        return 0

    lax.fori_loop(0, SECTIONS - 1, forward, 0)

    acc = jnp.zeros((ROWS, R), jnp.float32)
    for c in range(E // STEP):
        at = slice(c * STEP, (c + 1) * STEP)
        rows = target[:, at]
        grad[:, at] = rows
        acc += nt_dot(rows, out_part(SECTIONS - 1, c))
    hid[...] = acc

    def backward(i, _):
        k = SECTIONS - 1 - i
        p = pre[k]
        inv = root[k]
        squash = jax.nn.sigmoid(p)
        act = hid[...] * squash * (1.0 + p * (1.0 - squash))
        inner = jnp.sum(act * p, axis=1, keepdims=True) * (1.0 / E)
        scaled = (inv * act).astype(jnp.bfloat16)
        back = inv * inv * inner
        wide = jnp.concatenate([back, back], axis=1)

        @pl.when(k == place[0])
        def _():
            hidden = (p * squash).astype(jnp.bfloat16)
            for c in range(E // STEP):
                at = slice(c * STEP, (c + 1) * STEP)
                part = tn_dot(hidden, grad[:, at]).astype(jnp.bfloat16)
                staged[2 * c] = part[:, :LANES]
                staged[2 * c + 1] = part[:, LANES:]
                part = tn_dot(kept[k, :, at], scaled).astype(jnp.bfloat16)
                grad_in[c * STEP // 8 : (c + 1) * STEP // 8] = part.reshape(STEP // 8, 8, R)

        @pl.when(k > 0)
        def _():
            acc = jnp.zeros((ROWS, R), jnp.float32)
            for c in range(E // STEP):
                at = slice(c * STEP, (c + 1) * STEP)
                rows = grad[:, at].astype(jnp.float32) + nt_dot(scaled, w_in[k, at])
                rows = (rows - wide * kept[k, :, at].astype(jnp.float32)).astype(jnp.bfloat16)
                grad[:, at] = rows
                acc += nt_dot(rows, out_part(k - 1, c))
            hid[...] = acc

        return 0

    lax.fori_loop(0, SECTIONS, backward, 0)
    for swapped in range(2):
        into_in, into_out = (kept_out, sent_out) if swapped == 0 else (sent_out, kept_out)

        @pl.when(core == swapped)
        def _():
            stores = []
            for z in range(RINGS):
                at = (z % 4, z // 4)
                stores.append(
                    pltpu.make_async_copy(
                        grad_in.at[pl.ds(z * COLS, COLS)], into_in.at[at], out_sems.at[0, z]
                    )
                )
                stores.append(
                    pltpu.make_async_copy(
                        staged.at[:, pl.ds(z * 8, 8), :], into_out.at[at], out_sems.at[1, z]
                    )
                )
            for c in stores:
                c.start()
            for c in stores:
                c.wait()


def run_chain(place, stream, target, own, rest, quarters):
    whole = pl.BlockSpec(memory_space=pltpu.VMEM)
    anywhere = pl.BlockSpec(memory_space=pl.ANY)
    parts = []
    for part in (own, rest, *quarters):
        blocks, rings = part.shape[:2]
        parts += [part.reshape(blocks, rings * 2 * TILE_ROWS, R), part]
    piece = jax.ShapeDtypeStruct((4, 4, COLS, 8, LANES), jnp.bfloat16)
    return pl.pallas_call(
        chain,
        out_shape=(piece, piece),
        in_specs=[pl.BlockSpec(memory_space=pltpu.SMEM), whole, whole] + len(parts) * [anywhere],
        out_specs=(anywhere, anywhere),
        scratch_shapes=[
            pltpu.VMEM((SECTIONS, E, R), jnp.bfloat16),
            pltpu.VMEM((SECTIONS, COLS, R, LANES), jnp.bfloat16),
            pltpu.VMEM((SECTIONS, ROWS, E), jnp.bfloat16),
            pltpu.VMEM((ROWS, E), jnp.bfloat16),
            pltpu.VMEM((SECTIONS, ROWS, R), jnp.float32),
            pltpu.VMEM((SECTIONS, ROWS, LANES), jnp.float32),
            pltpu.VMEM((ROWS, R), jnp.float32),
            pltpu.VMEM((E // 8, 8, R), jnp.bfloat16),
            pltpu.VMEM((COLS, R, LANES), jnp.bfloat16),
            pltpu.SemaphoreType.DMA((SECTIONS, 19)),
            pltpu.SemaphoreType.DMA((2, RINGS)),
        ],
        compiler_params=pltpu.CompilerParams(vmem_limit_bytes=60 * 1024 * 1024),
    )(place, stream, target, *parts)


def swap_cores(x):
    return lax.ppermute(x, "dp_1", [(0, 1), (1, 0)])


def update(weight, grad, moment, variance, factor):
    scaled = factor * grad
    moment = BETA_ONE * moment + (1.0 - BETA_ONE) * scaled
    variance = BETA_TWO * variance + (1.0 - BETA_TWO) * scaled * scaled
    weight = weight.astype(jnp.float32) - STEP_RATE * moment / (jnp.sqrt(variance) + ADAM_EPS)
    return (weight[None], moment[None], variance[None])


def shards(
    stream_in,
    cotangent,
    norm_gain,
    weight_in,
    weight_out,
    moment_in,
    variance_in,
    moment_out,
    variance_out,
):
    section = lax.axis_index(SECTION)
    ring = lax.axis_index(RING)
    core = lax.axis_index("dp_1")
    first = core == 0
    dp = lax.axis_index(DP)
    in_slice = weight_in[0]
    out_slice = weight_out[0]
    own_rows = in_slice.shape[0]
    gain = lax.dynamic_slice_in_dim(norm_gain[0], dp * own_rows, own_rows).astype(jnp.float32)

    in_part = (in_slice.astype(jnp.float32) * gain[:, None]).astype(jnp.bfloat16)
    in_part = in_part.reshape(COLS, 4, LANES)
    out_part = out_slice.reshape(4, COLS, LANES).transpose(1, 0, 2)
    other = swap_cores(jnp.where(first, out_part, in_part))
    of_in = jnp.concatenate([in_part, other], axis=0).reshape(COLS, 8, LANES)
    of_out = jnp.concatenate([other, out_part], axis=1)
    pair = jnp.where(first, of_in, of_out)
    column = lax.all_gather(pair[None], RING, axis=0, tiled=True)
    plane = SECTION + ("dp_1",)
    own = jnp.where(ring % 2 == 0, column[:4], column[4:8])
    own = lax.all_gather(own[None], plane, axis=0, tiled=True)
    rest = lax.all_gather(column[8:][None], plane, axis=0, tiled=True)
    blocks = own.shape[0] // 4
    quarters = []
    for side, by in enumerate((1, -1)):
        quarter = lax.dynamic_slice_in_dim(own, (2 * core + side) * blocks, blocks)
        quarters.append(
            lax.ppermute(quarter, RING, [(i, (i + by) % RINGS) for i in range(RINGS)])
        )
    quarters += [swap_cores(quarter) for quarter in quarters]

    place = jnp.stack([section, core, ring % 2]).astype(jnp.int32)
    kept, sent = run_chain(
        place, stream_in.reshape(ROWS, E), cotangent.reshape(ROWS, E), own, rest, quarters
    )
    total = kept.astype(jnp.float32) + swap_cores(sent).astype(jnp.float32)
    for axis in ("ring_1", "ring_0"):
        pieces = lax.all_to_all(total.astype(jnp.bfloat16), axis, 0, 0, tiled=True)
        total = jnp.sum(pieces.astype(jnp.float32), axis=0)
    chip_gain = lax.dynamic_slice_in_dim(norm_gain[0], ring * 2 * own_rows, 2 * own_rows)
    total = total.reshape(2 * own_rows, LANES)
    total = total * jnp.where(first, chip_gain.astype(jnp.float32), 1.0)[:, None]
    chip_sum = jnp.sum(total * total)
    device_count = lax.axis_size(EVERY)
    sums = jnp.broadcast_to(chip_sum, (device_count, 1, LANES))
    sums = lax.all_to_all(sums, EVERY, 0, 0, tiled=True)
    norm_total = jnp.sum(sums[:, 0, 0])

    as_in = total.reshape(2, own_rows, LANES)
    as_out = total.reshape(COLS, 2, 4, LANES)
    mine = jnp.where(first, as_in[0], as_out[:, 1].reshape(own_rows, LANES))
    theirs = jnp.where(first, as_in[1], as_out[:, 0].reshape(own_rows, LANES))
    arrived = swap_cores(theirs)
    grad_w_in = jnp.where(first, mine, arrived)
    grad_w_out = jnp.where(first, arrived, mine).reshape(COLS, 4, LANES)
    grad_w_out = grad_w_out.transpose(1, 0, 2).reshape(4, E)

    count_all = 2.0 * E * R * SECTIONS
    factor = jnp.minimum(1.0, lax.rsqrt(norm_total / count_all + CLIP_EPS))
    new_in, new_moment_in, new_variance_in = update(
        in_slice, grad_w_in, moment_in[0], variance_in[0], factor
    )
    new_out, new_moment_out, new_variance_out = update(
        out_slice, grad_w_out, moment_out[0], variance_out[0], factor
    )
    return (new_in, new_moment_in, new_variance_in, new_out, new_moment_out, new_variance_out)


def solution(mesh):
    finer = Mesh(mesh.devices.reshape(4, 4, 4, 4, 2), EVERY)
    placed = (P(None, DP, None), P(None, DP, None), P(SECTION, None)) + 6 * (
        P(SECTION, DP, None),
    )
    return jax.shard_map(
        shards, mesh=finer, in_specs=placed, out_specs=6 * (P(SECTION, DP, None),), check_vma=False
    )
```

```python
import jax
import jax.numpy as jnp
from jax import lax
from jax.experimental import pallas as pl
from jax.experimental.pallas import tpu as pltpu
from jax.sharding import Mesh
from jax.sharding import PartitionSpec as P

E = 3584
R = 128
SECTIONS = 16
ROWS = 128
STEP = 256
LANES = 128
COLS = E // LANES
RINGS = 16
TILE_ROWS = E // 32
SECTION = ("section_0", "section_1")
RING = ("ring_0", "ring_1")
DP = RING + ("dp_1",)
EVERY = SECTION + DP
PLANE = SECTION + ("dp_1",)
SHARED = 10
DEPTH = 5

NORM_EPS = 1e-06
BETA_ONE = 0.9
BETA_TWO = 0.95
STEP_RATE = 0.01
ADAM_EPS = 1e-08
CLIP_EPS = 1e-06


def nt_dot(left, right):
    return lax.dot_general(
        left, right, (((1,), (1,)), ((), ())), preferred_element_type=jnp.float32
    )


def tn_dot(left, right):
    return lax.dot_general(
        left, right, (((0,), (0,)), ((), ())), preferred_element_type=jnp.float32
    )


def chain(
    place, stream, target, shared, shared_tiles, *more
):
    own = [more[2 * i : 2 * i + 2] for i in range(5)]
    sibling = [more[2 * i : 2 * i + 2] for i in range(5, 10)]
    (
        kept_out, sent_out, w_in, w_out, kept, grad, pre, root, hid, grad_in, staged, sems, out_sems
    ) = more[20:]
    section = place[0]
    core = place[1]

    def in_copy(k, flat, at, ring, sem):
        rows = pl.ds(ring * 2 * TILE_ROWS, flat.shape[1])
        return [pltpu.make_async_copy(flat.at[at], w_in.at[k, rows, :], sems.at[k, sem])]

    def out_copies(k, tiles, at, ring, sem):
        return [
            pltpu.make_async_copy(
                tiles.at[at, z], w_out.at[k, :, pl.ds((ring + z) * 8, 8), :], sems.at[k, sem + z]
            )
            for z in range(tiles.shape[1])
        ]

    def shared_copies(k):
        return in_copy(k, shared, 2 * k, 0, 0) + out_copies(k, shared_tiles, 2 * k + 1, 0, 2)

    def far_copies(k, in_source, out_source):
        flat, _, in_at = in_source
        _, tiles, out_at = out_source
        return in_copy(k, flat, in_at, SHARED, 1) + out_copies(k, tiles, out_at, SHARED, 2 + SHARED)

    def block(arrays, along, across):
        place_of = {3: 0, 1: 1, 2: 2}
        if along == 0:
            return (*arrays[0], 0 if across == 0 else 1 + place_of[across])
        if across == 0:
            return (*arrays[1], place_of[along])
        return (*arrays[2 + place_of[across]], place_of[along])

    def start(k, _):
        for c in shared_copies(k):
            c.start()
        off_x = (k // 4 - section // 4) % 4
        off_y = (k % 4 - section % 4) % 4
        for side in range(2):
            first, second = (own, sibling) if side == 0 else (sibling, own)

            @pl.when(core == side)
            def _():
                for x in range(4):

                    @pl.when(off_x == x)
                    def _():
                        for y in range(4):

                            @pl.when(off_y == y)
                            def _():
                                for c in far_copies(k, block(first, x, y), block(second, y, x)):
                                    c.start()

        return 0

    def wait(k):
        for c in shared_copies(k) + far_copies(k, (*own[0], 0), (*own[0], 0)):
            c.wait()

    lax.fori_loop(0, DEPTH, start, 0)
    kept[0] = stream[...]

    def out_part(k, c):
        return jnp.concatenate([w_out[k, 2 * c], w_out[k, 2 * c + 1]], axis=1)

    def squares(values):
        return values[:, :LANES] * values[:, :LANES] + values[:, LANES:] * values[:, LANES:]

    def finish(k, acc, total):
        mean = jnp.sum(total, axis=1, keepdims=True) * (1.0 / E)
        inv = lax.rsqrt(mean + NORM_EPS)
        pre[k] = acc * inv
        root[k] = jnp.broadcast_to(inv, (ROWS, LANES))

    wait(0)
    acc = jnp.zeros((ROWS, R), jnp.float32)
    total = jnp.zeros((ROWS, LANES), jnp.float32)
    for c in range(E // STEP):
        rows = stream[:, c * STEP : (c + 1) * STEP]
        total += squares(rows.astype(jnp.float32))
        acc += jnp.dot(
            rows, w_in[0, c * STEP : (c + 1) * STEP], preferred_element_type=jnp.float32
        )
    finish(0, acc, total)

    def forward(k, _):
        wait(k + 1)

        @pl.when(k + DEPTH < SECTIONS)
        def _():
            start(k + DEPTH, 0)

        p = pre[k]
        hidden = (p * jax.nn.sigmoid(p)).astype(jnp.bfloat16)
        acc = jnp.zeros((ROWS, R), jnp.float32)
        total = jnp.zeros((ROWS, LANES), jnp.float32)
        for c in range(E // STEP):
            at = slice(c * STEP, (c + 1) * STEP)
            rows = kept[k, :, at].astype(jnp.float32) + jnp.dot(
                hidden, out_part(k, c), preferred_element_type=jnp.float32
            )
            rows = rows.astype(jnp.bfloat16)
            kept[k + 1, :, at] = rows
            total += squares(rows.astype(jnp.float32))
            acc += jnp.dot(rows, w_in[k + 1, at], preferred_element_type=jnp.float32)
        finish(k + 1, acc, total)
        return 0

    lax.fori_loop(0, SECTIONS - 1, forward, 0)

    acc = jnp.zeros((ROWS, R), jnp.float32)
    for c in range(E // STEP):
        at = slice(c * STEP, (c + 1) * STEP)
        rows = target[:, at]
        grad[:, at] = rows
        acc += nt_dot(rows, out_part(SECTIONS - 1, c))
    hid[...] = acc

    def backward(i, _):
        k = SECTIONS - 1 - i
        p = pre[k]
        inv = root[k]
        squash = jax.nn.sigmoid(p)
        act = hid[...] * squash * (1.0 + p * (1.0 - squash))
        inner = jnp.sum(act * p, axis=1, keepdims=True) * (1.0 / E)
        scaled = (inv * act).astype(jnp.bfloat16)
        back = inv * inv * inner
        wide = jnp.concatenate([back, back], axis=1)

        @pl.when(k == place[0])
        def _():
            hidden = (p * squash).astype(jnp.bfloat16)
            for c in range(E // STEP):
                at = slice(c * STEP, (c + 1) * STEP)
                part = tn_dot(hidden, grad[:, at]).astype(jnp.bfloat16)
                staged[2 * c] = part[:, :LANES]
                staged[2 * c + 1] = part[:, LANES:]
                part = tn_dot(kept[k, :, at], scaled).astype(jnp.bfloat16)
                grad_in[c * STEP // 8 : (c + 1) * STEP // 8] = part.reshape(STEP // 8, 8, R)

        @pl.when(k > 0)
        def _():
            acc = jnp.zeros((ROWS, R), jnp.float32)
            for c in range(E // STEP):
                at = slice(c * STEP, (c + 1) * STEP)
                rows = grad[:, at].astype(jnp.float32) + nt_dot(scaled, w_in[k, at])
                rows = (rows - wide * kept[k, :, at].astype(jnp.float32)).astype(jnp.bfloat16)
                grad[:, at] = rows
                acc += nt_dot(rows, out_part(k - 1, c))
            hid[...] = acc

        return 0

    lax.fori_loop(0, SECTIONS, backward, 0)
    for swapped in range(2):
        into_in, into_out = (kept_out, sent_out) if swapped == 0 else (sent_out, kept_out)

        @pl.when(core == swapped)
        def _():
            stores = []
            for z in range(RINGS):
                at = (z % 4, z // 4)
                stores.append(
                    pltpu.make_async_copy(
                        grad_in.at[pl.ds(z * COLS, COLS)], into_in.at[at], out_sems.at[0, z]
                    )
                )
                stores.append(
                    pltpu.make_async_copy(
                        staged.at[:, pl.ds(z * 8, 8), :], into_out.at[at], out_sems.at[1, z]
                    )
                )
            for c in stores:
                c.start()
            for c in stores:
                c.wait()


def run_chain(place, stream, target, parts_of):
    whole = pl.BlockSpec(memory_space=pltpu.VMEM)
    anywhere = pl.BlockSpec(memory_space=pl.ANY)
    parts = []
    for part in parts_of:
        blocks, rings = part.shape[:2]
        parts += [part.reshape(blocks, rings * 2 * TILE_ROWS, R), part]
    piece = jax.ShapeDtypeStruct((4, 4, COLS, 8, LANES), jnp.bfloat16)
    return pl.pallas_call(
        chain,
        out_shape=(piece, piece),
        in_specs=[pl.BlockSpec(memory_space=pltpu.SMEM), whole, whole] + len(parts) * [anywhere],
        out_specs=(anywhere, anywhere),
        scratch_shapes=[
            pltpu.VMEM((SECTIONS, E, R), jnp.bfloat16),
            pltpu.VMEM((SECTIONS, COLS, R, LANES), jnp.bfloat16),
            pltpu.VMEM((SECTIONS, ROWS, E), jnp.bfloat16),
            pltpu.VMEM((ROWS, E), jnp.bfloat16),
            pltpu.VMEM((SECTIONS, ROWS, R), jnp.float32),
            pltpu.VMEM((SECTIONS, ROWS, LANES), jnp.float32),
            pltpu.VMEM((ROWS, R), jnp.float32),
            pltpu.VMEM((E // 8, 8, R), jnp.bfloat16),
            pltpu.VMEM((COLS, R, LANES), jnp.bfloat16),
            pltpu.SemaphoreType.DMA((SECTIONS, 2 + RINGS)),
            pltpu.SemaphoreType.DMA((2, RINGS)),
        ],
        compiler_params=pltpu.CompilerParams(vmem_limit_bytes=60 * 1024 * 1024),
    )(place, stream, target, *parts)


def shifted(x, along, across):
    pairs = []
    for i in range(4):
        for j in range(4):
            for core, (di, dj) in enumerate(((along, across), (across, along))):
                target = 4 * ((i + di) % 4) + (j + dj) % 4
                pairs.append((2 * (4 * i + j) + core, 2 * target + core))
    return lax.ppermute(x, PLANE, pairs)


def swap_cores(x):
    return lax.ppermute(x, "dp_1", [(0, 1), (1, 0)])


def update(weight, grad, moment, variance, factor):
    scaled = factor * grad
    moment = BETA_ONE * moment + (1.0 - BETA_ONE) * scaled
    variance = BETA_TWO * variance + (1.0 - BETA_TWO) * scaled * scaled
    weight = weight.astype(jnp.float32) - STEP_RATE * moment / (jnp.sqrt(variance) + ADAM_EPS)
    return (weight[None], moment[None], variance[None])


def shards(
    stream_in,
    cotangent,
    norm_gain,
    weight_in,
    weight_out,
    moment_in,
    variance_in,
    moment_out,
    variance_out,
):
    section = lax.axis_index(SECTION)
    ring = lax.axis_index(RING)
    core = lax.axis_index("dp_1")
    first = core == 0
    dp = lax.axis_index(DP)
    in_slice = weight_in[0]
    out_slice = weight_out[0]
    own_rows = in_slice.shape[0]
    gain = lax.dynamic_slice_in_dim(norm_gain[0], dp * own_rows, own_rows).astype(jnp.float32)

    in_part = (in_slice.astype(jnp.float32) * gain[:, None]).astype(jnp.bfloat16)
    in_part = in_part.reshape(COLS, 4, LANES)
    out_part = out_slice.reshape(4, COLS, LANES).transpose(1, 0, 2)
    other = swap_cores(jnp.where(first, out_part, in_part))
    of_in = jnp.concatenate([in_part, other], axis=0).reshape(COLS, 8, LANES)
    of_out = jnp.concatenate([other, out_part], axis=1)
    pair = jnp.where(first, of_in, of_out)
    column = lax.all_gather(pair[None], RING, axis=0, tiled=True)
    shared = lax.all_gather(column[:SHARED][None], PLANE, axis=0, tiled=True)
    block = column[SHARED:][None]
    shifts = (1, -1, 2)
    along = [shifted(block, by, 0) for by in shifts]
    across = [shifted(block, 0, by) for by in shifts]
    row = jnp.concatenate(along, axis=0)
    near = jnp.concatenate([block] + across, axis=0)
    row, near = lax.optimization_barrier((row, near))
    up, down = shifted(row, 0, 1), shifted(row, 0, -1)
    half = row.shape[1] // 2
    beyond = jnp.concatenate([shifted(up[:, :half], 0, 1), shifted(down[:, half:], 0, -1)], axis=1)
    own = [near, row, up, down, beyond]
    sibling = [swap_cores(part) for part in own]

    place = jnp.stack([section, core]).astype(jnp.int32)
    kept, sent = run_chain(
        place, stream_in.reshape(ROWS, E), cotangent.reshape(ROWS, E), [shared] + own + sibling
    )
    total = kept.astype(jnp.float32) + swap_cores(sent).astype(jnp.float32)
    for axis in ("ring_1", "ring_0"):
        pieces = lax.all_to_all(total.astype(jnp.bfloat16), axis, 0, 0, tiled=True)
        total = jnp.sum(pieces.astype(jnp.float32), axis=0)
    chip_gain = lax.dynamic_slice_in_dim(norm_gain[0], ring * 2 * own_rows, 2 * own_rows)
    total = total.reshape(2 * own_rows, LANES)
    total = total * jnp.where(first, chip_gain.astype(jnp.float32), 1.0)[:, None]
    chip_sum = jnp.sum(total * total)
    device_count = lax.axis_size(EVERY)
    sums = jnp.broadcast_to(chip_sum, (device_count, 1, LANES))
    sums = lax.all_to_all(sums, EVERY, 0, 0, tiled=True)
    norm_total = jnp.sum(sums[:, 0, 0])

    as_in = total.reshape(2, own_rows, LANES)
    as_out = total.reshape(COLS, 2, 4, LANES)
    mine = jnp.where(first, as_in[0], as_out[:, 1].reshape(own_rows, LANES))
    theirs = jnp.where(first, as_in[1], as_out[:, 0].reshape(own_rows, LANES))
    arrived = swap_cores(theirs)
    grad_w_in = jnp.where(first, mine, arrived)
    grad_w_out = jnp.where(first, arrived, mine).reshape(COLS, 4, LANES)
    grad_w_out = grad_w_out.transpose(1, 0, 2).reshape(4, E)

    count_all = 2.0 * E * R * SECTIONS
    factor = jnp.minimum(1.0, lax.rsqrt(norm_total / count_all + CLIP_EPS))
    new_in, new_moment_in, new_variance_in = update(
        in_slice, grad_w_in, moment_in[0], variance_in[0], factor
    )
    new_out, new_moment_out, new_variance_out = update(
        out_slice, grad_w_out, moment_out[0], variance_out[0], factor
    )
    return (new_in, new_moment_in, new_variance_in, new_out, new_moment_out, new_variance_out)


def solution(mesh):
    finer = Mesh(mesh.devices.reshape(4, 4, 4, 4, 2), EVERY)
    placed = (P(None, DP, None), P(None, DP, None), P(SECTION, None)) + 6 * (
        P(SECTION, DP, None),
    )
    return jax.shard_map(
        shards, mesh=finer, in_specs=placed, out_specs=6 * (P(SECTION, DP, None),), check_vma=False
    )
```

```python
import jax
import jax.numpy as jnp
from jax import lax
from jax.experimental import pallas as pl
from jax.experimental.pallas import tpu as pltpu
from jax.sharding import Mesh
from jax.sharding import PartitionSpec as P

E = 3584
R = 128
SECTIONS = 16
ROWS = 128
STEP = 256
LANES = 128
COLS = E // LANES
RINGS = 16
TILE_ROWS = E // 32
SECTION = ("section_0", "section_1")
RING = ("ring_0", "ring_1")
DP = RING + ("dp_1",)
EVERY = SECTION + DP
PLANE = SECTION + ("dp_1",)
SHARED = 8
DEPTH = 5

NORM_EPS = 1e-06
BETA_ONE = 0.9
BETA_TWO = 0.95
STEP_RATE = 0.01
ADAM_EPS = 1e-08
CLIP_EPS = 1e-06


def nt_dot(left, right):
    return lax.dot_general(
        left, right, (((1,), (1,)), ((), ())), preferred_element_type=jnp.float32
    )


def tn_dot(left, right):
    return lax.dot_general(
        left, right, (((0,), (0,)), ((), ())), preferred_element_type=jnp.float32
    )


def chain(
    place, stream, target, shared, shared_tiles, *more
):
    own = [more[2 * i : 2 * i + 2] for i in range(4)]
    sibling = [more[2 * i : 2 * i + 2] for i in range(4, 8)]
    (
        kept_out, sent_out, w_in, w_out, kept, grad, pre, root, hid, grad_in, staged, sems, out_sems
    ) = more[16:]
    section = place[0]
    core = place[1]

    def in_copy(k, flat, at, ring, sem):
        rows = pl.ds(ring * 2 * TILE_ROWS, flat.shape[1])
        return [pltpu.make_async_copy(flat.at[at], w_in.at[k, rows, :], sems.at[k, sem])]

    def out_copies(k, tiles, at, ring, sem):
        return [
            pltpu.make_async_copy(
                tiles.at[at, z], w_out.at[k, :, pl.ds((ring + z) * 8, 8), :], sems.at[k, sem + z]
            )
            for z in range(tiles.shape[1])
        ]

    def shared_copies(k):
        return in_copy(k, shared, 2 * k, 0, 0) + out_copies(k, shared_tiles, 2 * k + 1, 0, 2)

    def far_copies(k, in_source, out_source):
        flat, _, in_at = in_source
        _, tiles, out_at = out_source
        return in_copy(k, flat, in_at, SHARED, 1) + out_copies(k, tiles, out_at, SHARED, 2 + SHARED)

    def block(arrays, along, across):
        place_of = {0: 0, 3: 1, 1: 2, 2: 3}
        return (*arrays[place_of[across]], place_of[along])

    def start(k, _):
        for c in shared_copies(k):
            c.start()
        off_x = (k // 4 - section // 4) % 4
        off_y = (k % 4 - section % 4) % 4
        for side in range(2):
            first, second = (own, sibling) if side == 0 else (sibling, own)

            @pl.when(core == side)
            def _():
                for x in range(4):

                    @pl.when(off_x == x)
                    def _():
                        for y in range(4):

                            @pl.when(off_y == y)
                            def _():
                                for c in far_copies(k, block(first, x, y), block(second, y, x)):
                                    c.start()

        return 0

    def wait(k):
        for c in shared_copies(k) + far_copies(k, (*own[0], 0), (*own[0], 0)):
            c.wait()

    lax.fori_loop(0, DEPTH, start, 0)
    kept[0] = stream[...]

    def out_part(k, c):
        return jnp.concatenate([w_out[k, 2 * c], w_out[k, 2 * c + 1]], axis=1)

    def squares(values):
        return values[:, :LANES] * values[:, :LANES] + values[:, LANES:] * values[:, LANES:]

    def finish(k, acc, total):
        mean = jnp.sum(total, axis=1, keepdims=True) * (1.0 / E)
        inv = lax.rsqrt(mean + NORM_EPS)
        pre[k] = acc * inv
        root[k] = jnp.broadcast_to(inv, (ROWS, LANES))

    wait(0)
    acc = jnp.zeros((ROWS, R), jnp.float32)
    total = jnp.zeros((ROWS, LANES), jnp.float32)
    for c in range(E // STEP):
        rows = stream[:, c * STEP : (c + 1) * STEP]
        total += squares(rows.astype(jnp.float32))
        acc += jnp.dot(
            rows, w_in[0, c * STEP : (c + 1) * STEP], preferred_element_type=jnp.float32
        )
    finish(0, acc, total)

    def forward(k, _):
        wait(k + 1)

        @pl.when(k + DEPTH < SECTIONS)
        def _():
            start(k + DEPTH, 0)

        p = pre[k]
        hidden = (p * jax.nn.sigmoid(p)).astype(jnp.bfloat16)
        acc = jnp.zeros((ROWS, R), jnp.float32)
        total = jnp.zeros((ROWS, LANES), jnp.float32)
        for c in range(E // STEP):
            at = slice(c * STEP, (c + 1) * STEP)
            rows = kept[k, :, at].astype(jnp.float32) + jnp.dot(
                hidden, out_part(k, c), preferred_element_type=jnp.float32
            )
            rows = rows.astype(jnp.bfloat16)
            kept[k + 1, :, at] = rows
            total += squares(rows.astype(jnp.float32))
            acc += jnp.dot(rows, w_in[k + 1, at], preferred_element_type=jnp.float32)
        finish(k + 1, acc, total)
        return 0

    lax.fori_loop(0, SECTIONS - 1, forward, 0)

    acc = jnp.zeros((ROWS, R), jnp.float32)
    for c in range(E // STEP):
        at = slice(c * STEP, (c + 1) * STEP)
        rows = target[:, at]
        grad[:, at] = rows
        acc += nt_dot(rows, out_part(SECTIONS - 1, c))
    hid[...] = acc

    def backward(i, _):
        k = SECTIONS - 1 - i
        p = pre[k]
        inv = root[k]
        squash = jax.nn.sigmoid(p)
        act = hid[...] * squash * (1.0 + p * (1.0 - squash))
        inner = jnp.sum(act * p, axis=1, keepdims=True) * (1.0 / E)
        scaled = (inv * act).astype(jnp.bfloat16)
        back = inv * inv * inner
        wide = jnp.concatenate([back, back], axis=1)

        @pl.when(k == place[0])
        def _():
            hidden = (p * squash).astype(jnp.bfloat16)
            for c in range(E // STEP):
                at = slice(c * STEP, (c + 1) * STEP)
                part = tn_dot(hidden, grad[:, at]).astype(jnp.bfloat16)
                staged[2 * c] = part[:, :LANES]
                staged[2 * c + 1] = part[:, LANES:]
                part = tn_dot(kept[k, :, at], scaled).astype(jnp.bfloat16)
                grad_in[c * STEP // 8 : (c + 1) * STEP // 8] = part.reshape(STEP // 8, 8, R)

        @pl.when(k > 0)
        def _():
            acc = jnp.zeros((ROWS, R), jnp.float32)
            for c in range(E // STEP):
                at = slice(c * STEP, (c + 1) * STEP)
                rows = grad[:, at].astype(jnp.float32) + nt_dot(scaled, w_in[k, at])
                rows = (rows - wide * kept[k, :, at].astype(jnp.float32)).astype(jnp.bfloat16)
                grad[:, at] = rows
                acc += nt_dot(rows, out_part(k - 1, c))
            hid[...] = acc

        return 0

    lax.fori_loop(0, SECTIONS, backward, 0)
    for swapped in range(2):
        into_in, into_out = (kept_out, sent_out) if swapped == 0 else (sent_out, kept_out)

        @pl.when(core == swapped)
        def _():
            stores = []
            for z in range(RINGS):
                at = (z % 4, z // 4)
                stores.append(
                    pltpu.make_async_copy(
                        grad_in.at[pl.ds(z * COLS, COLS)], into_in.at[at], out_sems.at[0, z]
                    )
                )
                stores.append(
                    pltpu.make_async_copy(
                        staged.at[:, pl.ds(z * 8, 8), :], into_out.at[at], out_sems.at[1, z]
                    )
                )
            for c in stores:
                c.start()
            for c in stores:
                c.wait()


def run_chain(place, stream, target, parts_of):
    whole = pl.BlockSpec(memory_space=pltpu.VMEM)
    anywhere = pl.BlockSpec(memory_space=pl.ANY)
    parts = []
    for part in parts_of:
        blocks, rings = part.shape[:2]
        parts += [part.reshape(blocks, rings * 2 * TILE_ROWS, R), part]
    piece = jax.ShapeDtypeStruct((4, 4, COLS, 8, LANES), jnp.bfloat16)
    return pl.pallas_call(
        chain,
        out_shape=(piece, piece),
        in_specs=[pl.BlockSpec(memory_space=pltpu.SMEM), whole, whole] + len(parts) * [anywhere],
        out_specs=(anywhere, anywhere),
        scratch_shapes=[
            pltpu.VMEM((SECTIONS, E, R), jnp.bfloat16),
            pltpu.VMEM((SECTIONS, COLS, R, LANES), jnp.bfloat16),
            pltpu.VMEM((SECTIONS, ROWS, E), jnp.bfloat16),
            pltpu.VMEM((ROWS, E), jnp.bfloat16),
            pltpu.VMEM((SECTIONS, ROWS, R), jnp.float32),
            pltpu.VMEM((SECTIONS, ROWS, LANES), jnp.float32),
            pltpu.VMEM((ROWS, R), jnp.float32),
            pltpu.VMEM((E // 8, 8, R), jnp.bfloat16),
            pltpu.VMEM((COLS, R, LANES), jnp.bfloat16),
            pltpu.SemaphoreType.DMA((SECTIONS, 2 + RINGS)),
            pltpu.SemaphoreType.DMA((2, RINGS)),
        ],
        compiler_params=pltpu.CompilerParams(vmem_limit_bytes=60 * 1024 * 1024),
    )(place, stream, target, *parts)


def shifted(x, along, across):
    pairs = []
    for i in range(4):
        for j in range(4):
            for core, (di, dj) in enumerate(((along, across), (across, along))):
                target = 4 * ((i + di) % 4) + (j + dj) % 4
                pairs.append((2 * (4 * i + j) + core, 2 * target + core))
    return lax.ppermute(x, PLANE, pairs)


def swap_cores(x):
    return lax.ppermute(x, "dp_1", [(0, 1), (1, 0)])


def update(weight, grad, moment, variance, factor):
    scaled = factor * grad
    moment = BETA_ONE * moment + (1.0 - BETA_ONE) * scaled
    variance = BETA_TWO * variance + (1.0 - BETA_TWO) * scaled * scaled
    weight = weight.astype(jnp.float32) - STEP_RATE * moment / (jnp.sqrt(variance) + ADAM_EPS)
    return (weight[None], moment[None], variance[None])


def shards(
    stream_in,
    cotangent,
    norm_gain,
    weight_in,
    weight_out,
    moment_in,
    variance_in,
    moment_out,
    variance_out,
):
    section = lax.axis_index(SECTION)
    ring = lax.axis_index(RING)
    core = lax.axis_index("dp_1")
    first = core == 0
    dp = lax.axis_index(DP)
    in_slice = weight_in[0]
    out_slice = weight_out[0]
    own_rows = in_slice.shape[0]
    gain = lax.dynamic_slice_in_dim(norm_gain[0], dp * own_rows, own_rows).astype(jnp.float32)

    in_part = (in_slice.astype(jnp.float32) * gain[:, None]).astype(jnp.bfloat16)
    in_part = in_part.reshape(COLS, 4, LANES)
    out_part = out_slice.reshape(4, COLS, LANES).transpose(1, 0, 2)
    other = swap_cores(jnp.where(first, out_part, in_part))
    of_in = jnp.concatenate([in_part, other], axis=0).reshape(COLS, 8, LANES)
    of_out = jnp.concatenate([other, out_part], axis=1)
    pair = jnp.where(first, of_in, of_out)
    column = lax.all_gather(pair[None], RING, axis=0, tiled=True)
    shared = lax.all_gather(column[:SHARED][None], PLANE, axis=0, tiled=True)
    block = column[SHARED:][None]
    row = lax.optimization_barrier(
        jnp.concatenate([block] + [shifted(block, by, 0) for by in (1, -1, 2)], axis=0)
    )
    up, down = shifted(row, 0, 1), shifted(row, 0, -1)
    half = row.shape[1] // 2
    beyond = jnp.concatenate([shifted(up[:, :half], 0, 1), shifted(down[:, half:], 0, -1)], axis=1)
    own = [row, up, down, beyond]
    sibling = [swap_cores(part) for part in own]

    place = jnp.stack([section, core]).astype(jnp.int32)
    kept, sent = run_chain(
        place, stream_in.reshape(ROWS, E), cotangent.reshape(ROWS, E), [shared] + own + sibling
    )
    total = kept.astype(jnp.float32) + swap_cores(sent).astype(jnp.float32)
    for axis in ("ring_1", "ring_0"):
        pieces = lax.all_to_all(total.astype(jnp.bfloat16), axis, 0, 0, tiled=True)
        total = jnp.sum(pieces.astype(jnp.float32), axis=0)
    chip_gain = lax.dynamic_slice_in_dim(norm_gain[0], ring * 2 * own_rows, 2 * own_rows)
    total = total.reshape(2 * own_rows, LANES)
    total = total * jnp.where(first, chip_gain.astype(jnp.float32), 1.0)[:, None]
    chip_sum = jnp.sum(total * total)
    device_count = lax.axis_size(EVERY)
    sums = jnp.broadcast_to(chip_sum, (device_count, 1, LANES))
    sums = lax.all_to_all(sums, EVERY, 0, 0, tiled=True)
    norm_total = jnp.sum(sums[:, 0, 0])

    as_in = total.reshape(2, own_rows, LANES)
    as_out = total.reshape(COLS, 2, 4, LANES)
    mine = jnp.where(first, as_in[0], as_out[:, 1].reshape(own_rows, LANES))
    theirs = jnp.where(first, as_in[1], as_out[:, 0].reshape(own_rows, LANES))
    arrived = swap_cores(theirs)
    grad_w_in = jnp.where(first, mine, arrived)
    grad_w_out = jnp.where(first, arrived, mine).reshape(COLS, 4, LANES)
    grad_w_out = grad_w_out.transpose(1, 0, 2).reshape(4, E)

    count_all = 2.0 * E * R * SECTIONS
    factor = jnp.minimum(1.0, lax.rsqrt(norm_total / count_all + CLIP_EPS))
    new_in, new_moment_in, new_variance_in = update(
        in_slice, grad_w_in, moment_in[0], variance_in[0], factor
    )
    new_out, new_moment_out, new_variance_out = update(
        out_slice, grad_w_out, moment_out[0], variance_out[0], factor
    )
    return (new_in, new_moment_in, new_variance_in, new_out, new_moment_out, new_variance_out)


def solution(mesh):
    finer = Mesh(mesh.devices.reshape(4, 4, 4, 4, 2), EVERY)
    placed = (P(None, DP, None), P(None, DP, None), P(SECTION, None)) + 6 * (
        P(SECTION, DP, None),
    )
    return jax.shard_map(
        shards, mesh=finer, in_specs=placed, out_specs=6 * (P(SECTION, DP, None),), check_vma=False
    )
```

```python
import jax
import jax.numpy as jnp
from jax import lax
from jax.experimental import pallas as pl
from jax.experimental.pallas import tpu as pltpu
from jax.sharding import Mesh
from jax.sharding import PartitionSpec as P

E = 3584
R = 128
SECTIONS = 16
ROWS = 128
STEP = 256
LANES = 128
COLS = E // LANES
RINGS = 16
TILE_ROWS = E // 32
SECTION = ("section_0", "section_1")
RING = ("ring_0", "ring_1")
DP = RING + ("dp_1",)
EVERY = SECTION + DP
PLANE = SECTION + ("dp_1",)
SHARED = 9
DEPTH = 5

NORM_EPS = 1e-06
BETA_ONE = 0.9
BETA_TWO = 0.95
STEP_RATE = 0.01
ADAM_EPS = 1e-08
CLIP_EPS = 1e-06


def nt_dot(left, right):
    return lax.dot_general(
        left, right, (((1,), (1,)), ((), ())), preferred_element_type=jnp.float32
    )


def tn_dot(left, right):
    return lax.dot_general(
        left, right, (((0,), (0,)), ((), ())), preferred_element_type=jnp.float32
    )


def chain(
    place, stream, target, shared, shared_tiles, *more
):
    own = [more[2 * i : 2 * i + 2] for i in range(5)]
    sibling = [more[2 * i : 2 * i + 2] for i in range(5, 10)]
    (
        kept_out, sent_out, w_in, w_out, kept, grad, pre, root, hid, grad_in, staged, sems, out_sems
    ) = more[20:]
    section = place[0]
    core = place[1]

    def in_copy(k, flat, at, ring, sem):
        rows = pl.ds(ring * 2 * TILE_ROWS, flat.shape[1])
        return [pltpu.make_async_copy(flat.at[at], w_in.at[k, rows, :], sems.at[k, sem])]

    def out_copies(k, tiles, at, ring, sem):
        return [
            pltpu.make_async_copy(
                tiles.at[at, z], w_out.at[k, :, pl.ds((ring + z) * 8, 8), :], sems.at[k, sem + z]
            )
            for z in range(tiles.shape[1])
        ]

    def shared_copies(k):
        return in_copy(k, shared, 2 * k, 0, 0) + out_copies(k, shared_tiles, 2 * k + 1, 0, 2)

    def far_copies(k, in_pieces, out_pieces):
        copies, ring = [], SHARED
        for flat, tiles, at in in_pieces:
            copies += in_copy(k, flat, at, ring, 1)
            ring += tiles.shape[1]
        ring = SHARED
        for _, tiles, at in out_pieces:
            copies += out_copies(k, tiles, at, ring, 2 + ring)
            ring += tiles.shape[1]
        return copies

    def block(arrays, along, across):
        at = {0: 0, 3: 1, 1: 2, 2: 3}[along]
        held = {0: [0], 3: [1], 1: [2], 2: [3, 4]}[across]
        return [(*arrays[i], at) for i in held]

    def start(k, _):
        for c in shared_copies(k):
            c.start()
        off_x = (k // 4 - section // 4) % 4
        off_y = (k % 4 - section % 4) % 4
        for side in range(2):
            first, second = (own, sibling) if side == 0 else (sibling, own)

            @pl.when(core == side)
            def _():
                for x in range(4):

                    @pl.when(off_x == x)
                    def _():
                        for y in range(4):

                            @pl.when(off_y == y)
                            def _():
                                for c in far_copies(k, block(first, x, y), block(second, y, x)):
                                    c.start()

        return 0

    def wait(k):
        for c in shared_copies(k) + far_copies(k, block(own, 0, 0), block(own, 0, 0)):
            c.wait()

    lax.fori_loop(0, DEPTH, start, 0)
    kept[0] = stream[...]

    def out_part(k, c):
        return jnp.concatenate([w_out[k, 2 * c], w_out[k, 2 * c + 1]], axis=1)

    def squares(values):
        return values[:, :LANES] * values[:, :LANES] + values[:, LANES:] * values[:, LANES:]

    def finish(k, acc, total):
        mean = jnp.sum(total, axis=1, keepdims=True) * (1.0 / E)
        inv = lax.rsqrt(mean + NORM_EPS)
        pre[k] = acc * inv
        root[k] = jnp.broadcast_to(inv, (ROWS, LANES))

    wait(0)
    acc = jnp.zeros((ROWS, R), jnp.float32)
    total = jnp.zeros((ROWS, LANES), jnp.float32)
    for c in range(E // STEP):
        rows = stream[:, c * STEP : (c + 1) * STEP]
        total += squares(rows.astype(jnp.float32))
        acc += jnp.dot(
            rows, w_in[0, c * STEP : (c + 1) * STEP], preferred_element_type=jnp.float32
        )
    finish(0, acc, total)

    def forward(k, _):
        wait(k + 1)

        @pl.when(k + DEPTH < SECTIONS)
        def _():
            start(k + DEPTH, 0)

        p = pre[k]
        hidden = (p * jax.nn.sigmoid(p)).astype(jnp.bfloat16)
        acc = jnp.zeros((ROWS, R), jnp.float32)
        total = jnp.zeros((ROWS, LANES), jnp.float32)
        for c in range(E // STEP):
            at = slice(c * STEP, (c + 1) * STEP)
            rows = kept[k, :, at].astype(jnp.float32) + jnp.dot(
                hidden, out_part(k, c), preferred_element_type=jnp.float32
            )
            rows = rows.astype(jnp.bfloat16)
            kept[k + 1, :, at] = rows
            total += squares(rows.astype(jnp.float32))
            acc += jnp.dot(rows, w_in[k + 1, at], preferred_element_type=jnp.float32)
        finish(k + 1, acc, total)
        return 0

    lax.fori_loop(0, SECTIONS - 1, forward, 0)

    acc = jnp.zeros((ROWS, R), jnp.float32)
    for c in range(E // STEP):
        at = slice(c * STEP, (c + 1) * STEP)
        rows = target[:, at]
        grad[:, at] = rows
        acc += nt_dot(rows, out_part(SECTIONS - 1, c))
    hid[...] = acc

    def backward(i, _):
        k = SECTIONS - 1 - i
        p = pre[k]
        inv = root[k]
        squash = jax.nn.sigmoid(p)
        act = hid[...] * squash * (1.0 + p * (1.0 - squash))
        inner = jnp.sum(act * p, axis=1, keepdims=True) * (1.0 / E)
        scaled = (inv * act).astype(jnp.bfloat16)
        back = inv * inv * inner
        wide = jnp.concatenate([back, back], axis=1)

        @pl.when(k == place[0])
        def _():
            hidden = (p * squash).astype(jnp.bfloat16)
            for c in range(E // STEP):
                at = slice(c * STEP, (c + 1) * STEP)
                part = tn_dot(hidden, grad[:, at]).astype(jnp.bfloat16)
                staged[2 * c] = part[:, :LANES]
                staged[2 * c + 1] = part[:, LANES:]
                part = tn_dot(kept[k, :, at], scaled).astype(jnp.bfloat16)
                grad_in[c * STEP // 8 : (c + 1) * STEP // 8] = part.reshape(STEP // 8, 8, R)

        @pl.when(k > 0)
        def _():
            acc = jnp.zeros((ROWS, R), jnp.float32)
            for c in range(E // STEP):
                at = slice(c * STEP, (c + 1) * STEP)
                rows = grad[:, at].astype(jnp.float32) + nt_dot(scaled, w_in[k, at])
                rows = (rows - wide * kept[k, :, at].astype(jnp.float32)).astype(jnp.bfloat16)
                grad[:, at] = rows
                acc += nt_dot(rows, out_part(k - 1, c))
            hid[...] = acc

        return 0

    lax.fori_loop(0, SECTIONS, backward, 0)
    for swapped in range(2):
        into_in, into_out = (kept_out, sent_out) if swapped == 0 else (sent_out, kept_out)

        @pl.when(core == swapped)
        def _():
            stores = []
            for z in range(RINGS):
                at = (z % 4, z // 4)
                stores.append(
                    pltpu.make_async_copy(
                        grad_in.at[pl.ds(z * COLS, COLS)], into_in.at[at], out_sems.at[0, z]
                    )
                )
                stores.append(
                    pltpu.make_async_copy(
                        staged.at[:, pl.ds(z * 8, 8), :], into_out.at[at], out_sems.at[1, z]
                    )
                )
            for c in stores:
                c.start()
            for c in stores:
                c.wait()


def run_chain(place, stream, target, parts_of):
    whole = pl.BlockSpec(memory_space=pltpu.VMEM)
    anywhere = pl.BlockSpec(memory_space=pl.ANY)
    parts = []
    for part in parts_of:
        blocks, rings = part.shape[:2]
        parts += [part.reshape(blocks, rings * 2 * TILE_ROWS, R), part]
    piece = jax.ShapeDtypeStruct((4, 4, COLS, 8, LANES), jnp.bfloat16)
    return pl.pallas_call(
        chain,
        out_shape=(piece, piece),
        in_specs=[pl.BlockSpec(memory_space=pltpu.SMEM), whole, whole] + len(parts) * [anywhere],
        out_specs=(anywhere, anywhere),
        scratch_shapes=[
            pltpu.VMEM((SECTIONS, E, R), jnp.bfloat16),
            pltpu.VMEM((SECTIONS, COLS, R, LANES), jnp.bfloat16),
            pltpu.VMEM((SECTIONS, ROWS, E), jnp.bfloat16),
            pltpu.VMEM((ROWS, E), jnp.bfloat16),
            pltpu.VMEM((SECTIONS, ROWS, R), jnp.float32),
            pltpu.VMEM((SECTIONS, ROWS, LANES), jnp.float32),
            pltpu.VMEM((ROWS, R), jnp.float32),
            pltpu.VMEM((E // 8, 8, R), jnp.bfloat16),
            pltpu.VMEM((COLS, R, LANES), jnp.bfloat16),
            pltpu.SemaphoreType.DMA((SECTIONS, 2 + RINGS)),
            pltpu.SemaphoreType.DMA((2, RINGS)),
        ],
        compiler_params=pltpu.CompilerParams(vmem_limit_bytes=60 * 1024 * 1024),
    )(place, stream, target, *parts)


def shifted(x, along, across):
    pairs = []
    for i in range(4):
        for j in range(4):
            for core, (di, dj) in enumerate(((along, across), (across, along))):
                target = 4 * ((i + di) % 4) + (j + dj) % 4
                pairs.append((2 * (4 * i + j) + core, 2 * target + core))
    return lax.ppermute(x, PLANE, pairs)


def swap_cores(x):
    return lax.ppermute(x, "dp_1", [(0, 1), (1, 0)])


def update(weight, grad, moment, variance, factor):
    scaled = factor * grad
    moment = BETA_ONE * moment + (1.0 - BETA_ONE) * scaled
    variance = BETA_TWO * variance + (1.0 - BETA_TWO) * scaled * scaled
    weight = weight.astype(jnp.float32) - STEP_RATE * moment / (jnp.sqrt(variance) + ADAM_EPS)
    return (weight[None], moment[None], variance[None])


def shards(
    stream_in,
    cotangent,
    norm_gain,
    weight_in,
    weight_out,
    moment_in,
    variance_in,
    moment_out,
    variance_out,
):
    section = lax.axis_index(SECTION)
    ring = lax.axis_index(RING)
    core = lax.axis_index("dp_1")
    first = core == 0
    dp = lax.axis_index(DP)
    in_slice = weight_in[0]
    out_slice = weight_out[0]
    own_rows = in_slice.shape[0]
    gain = lax.dynamic_slice_in_dim(norm_gain[0], dp * own_rows, own_rows).astype(jnp.float32)

    in_part = (in_slice.astype(jnp.float32) * gain[:, None]).astype(jnp.bfloat16)
    in_part = in_part.reshape(COLS, 4, LANES)
    out_part = out_slice.reshape(4, COLS, LANES).transpose(1, 0, 2)
    other = swap_cores(jnp.where(first, out_part, in_part))
    of_in = jnp.concatenate([in_part, other], axis=0).reshape(COLS, 8, LANES)
    of_out = jnp.concatenate([other, out_part], axis=1)
    pair = jnp.where(first, of_in, of_out)
    column = lax.all_gather(pair[None], RING, axis=0, tiled=True)
    shared = lax.all_gather(column[:SHARED][None], PLANE, axis=0, tiled=True)
    block = column[SHARED:][None]
    row = lax.optimization_barrier(
        jnp.concatenate([block] + [shifted(block, by, 0) for by in (1, -1, 2)], axis=0)
    )
    up, down = shifted(row, 0, 1), shifted(row, 0, -1)
    half = row.shape[1] // 2
    own = [row, up, down, shifted(up[:, :half], 0, 1), shifted(down[:, half:], 0, -1)]
    sibling = [swap_cores(part) for part in own]

    place = jnp.stack([section, core]).astype(jnp.int32)
    kept, sent = run_chain(
        place, stream_in.reshape(ROWS, E), cotangent.reshape(ROWS, E), [shared] + own + sibling
    )
    total = kept.astype(jnp.float32) + swap_cores(sent).astype(jnp.float32)
    for axis in ("ring_1", "ring_0"):
        pieces = lax.all_to_all(total.astype(jnp.bfloat16), axis, 0, 0, tiled=True)
        total = jnp.sum(pieces.astype(jnp.float32), axis=0)
    chip_gain = lax.dynamic_slice_in_dim(norm_gain[0], ring * 2 * own_rows, 2 * own_rows)
    total = total.reshape(2 * own_rows, LANES)
    total = total * jnp.where(first, chip_gain.astype(jnp.float32), 1.0)[:, None]
    chip_sum = jnp.sum(total * total)
    device_count = lax.axis_size(EVERY)
    sums = jnp.broadcast_to(chip_sum, (device_count, 1, LANES))
    sums = lax.all_to_all(sums, EVERY, 0, 0, tiled=True)
    norm_total = jnp.sum(sums[:, 0, 0])

    as_in = total.reshape(2, own_rows, LANES)
    as_out = total.reshape(COLS, 2, 4, LANES)
    mine = jnp.where(first, as_in[0], as_out[:, 1].reshape(own_rows, LANES))
    theirs = jnp.where(first, as_in[1], as_out[:, 0].reshape(own_rows, LANES))
    arrived = swap_cores(theirs)
    grad_w_in = jnp.where(first, mine, arrived)
    grad_w_out = jnp.where(first, arrived, mine).reshape(COLS, 4, LANES)
    grad_w_out = grad_w_out.transpose(1, 0, 2).reshape(4, E)

    count_all = 2.0 * E * R * SECTIONS
    factor = jnp.minimum(1.0, lax.rsqrt(norm_total / count_all + CLIP_EPS))
    new_in, new_moment_in, new_variance_in = update(
        in_slice, grad_w_in, moment_in[0], variance_in[0], factor
    )
    new_out, new_moment_out, new_variance_out = update(
        out_slice, grad_w_out, moment_out[0], variance_out[0], factor
    )
    return (new_in, new_moment_in, new_variance_in, new_out, new_moment_out, new_variance_out)


def solution(mesh):
    finer = Mesh(mesh.devices.reshape(4, 4, 4, 4, 2), EVERY)
    placed = (P(None, DP, None), P(None, DP, None), P(SECTION, None)) + 6 * (
        P(SECTION, DP, None),
    )
    return jax.shard_map(
        shards, mesh=finer, in_specs=placed, out_specs=6 * (P(SECTION, DP, None),), check_vma=False
    )
```

```python
import jax
import jax.numpy as jnp
from jax import lax
from jax.experimental import pallas as pl
from jax.experimental.pallas import tpu as pltpu
from jax.sharding import Mesh
from jax.sharding import PartitionSpec as P

E = 3584
R = 128
SECTIONS = 16
ROWS = 128
STEP = 256
LANES = 128
COLS = E // LANES
RINGS = 16
TILE_ROWS = E // 32
SECTION = ("section_0", "section_1")
RING = ("ring_0", "ring_1")
DP = RING + ("dp_1",)
EVERY = SECTION + DP
PLANE = SECTION + ("dp_1",)
SHARED = 9
DEPTH = 5

NORM_EPS = 1e-06
BETA_ONE = 0.9
BETA_TWO = 0.95
STEP_RATE = 0.01
ADAM_EPS = 1e-08
CLIP_EPS = 1e-06


def nt_dot(left, right):
    return lax.dot_general(
        left, right, (((1,), (1,)), ((), ())), preferred_element_type=jnp.float32
    )


def tn_dot(left, right):
    return lax.dot_general(
        left, right, (((0,), (0,)), ((), ())), preferred_element_type=jnp.float32
    )


def chain(
    place, stream, target, shared, shared_tiles, *more
):
    own = [more[2 * i : 2 * i + 2] for i in range(4)]
    sibling = [more[2 * i : 2 * i + 2] for i in range(4, 8)]
    (
        kept_out, sent_out, w_in, w_out, kept, grad, pre, root, hid, grad_in, staged, sems, out_sems
    ) = more[16:]
    section = place[0]
    core = place[1]

    def in_copy(k, flat, at, ring, sem):
        rows = pl.ds(ring * 2 * TILE_ROWS, flat.shape[1])
        return [pltpu.make_async_copy(flat.at[at], w_in.at[k, rows, :], sems.at[k, sem])]

    def out_copies(k, tiles, at, ring, sem):
        return [
            pltpu.make_async_copy(
                tiles.at[at, z], w_out.at[k, :, pl.ds((ring + z) * 8, 8), :], sems.at[k, sem + z]
            )
            for z in range(tiles.shape[1])
        ]

    def shared_copies(k):
        return in_copy(k, shared, 2 * k, 0, 0) + out_copies(k, shared_tiles, 2 * k + 1, 0, 2)

    def far_copies(k, in_source, out_source):
        flat, _, in_at = in_source
        _, tiles, out_at = out_source
        return in_copy(k, flat, in_at, SHARED, 1) + out_copies(k, tiles, out_at, SHARED, 2 + SHARED)

    def block(arrays, along, across):
        place_of = {0: 0, 3: 1, 1: 2, 2: 3}
        return (*arrays[place_of[across]], place_of[along])

    def start(k, _):
        for c in shared_copies(k):
            c.start()
        off_x = (k // 4 - section // 4) % 4
        off_y = (k % 4 - section % 4) % 4
        for side in range(2):
            first, second = (own, sibling) if side == 0 else (sibling, own)

            @pl.when(core == side)
            def _():
                for x in range(4):

                    @pl.when(off_x == x)
                    def _():
                        for y in range(4):

                            @pl.when(off_y == y)
                            def _():
                                for c in far_copies(k, block(first, x, y), block(second, y, x)):
                                    c.start()

        return 0

    def wait(k):
        for c in shared_copies(k) + far_copies(k, (*own[0], 0), (*own[0], 0)):
            c.wait()

    lax.fori_loop(0, DEPTH, start, 0)
    kept[0] = stream[...]

    def out_part(k, c):
        return jnp.concatenate([w_out[k, 2 * c], w_out[k, 2 * c + 1]], axis=1)

    def squares(values):
        return values[:, :LANES] * values[:, :LANES] + values[:, LANES:] * values[:, LANES:]

    def finish(k, acc, total):
        mean = jnp.sum(total, axis=1, keepdims=True) * (1.0 / E)
        inv = lax.rsqrt(mean + NORM_EPS)
        pre[k] = acc * inv
        root[k] = jnp.broadcast_to(inv, (ROWS, LANES))

    wait(0)
    acc = jnp.zeros((ROWS, R), jnp.float32)
    total = jnp.zeros((ROWS, LANES), jnp.float32)
    for c in range(E // STEP):
        rows = stream[:, c * STEP : (c + 1) * STEP]
        total += squares(rows.astype(jnp.float32))
        acc += jnp.dot(
            rows, w_in[0, c * STEP : (c + 1) * STEP], preferred_element_type=jnp.float32
        )
    finish(0, acc, total)

    def forward(k, _):
        wait(k + 1)

        @pl.when(k + DEPTH < SECTIONS)
        def _():
            start(k + DEPTH, 0)

        p = pre[k]
        hidden = (p * jax.nn.sigmoid(p)).astype(jnp.bfloat16)
        acc = jnp.zeros((ROWS, R), jnp.float32)
        total = jnp.zeros((ROWS, LANES), jnp.float32)
        for c in range(E // STEP):
            at = slice(c * STEP, (c + 1) * STEP)
            rows = kept[k, :, at].astype(jnp.float32) + jnp.dot(
                hidden, out_part(k, c), preferred_element_type=jnp.float32
            )
            rows = rows.astype(jnp.bfloat16)
            kept[k + 1, :, at] = rows
            total += squares(rows.astype(jnp.float32))
            acc += jnp.dot(rows, w_in[k + 1, at], preferred_element_type=jnp.float32)
        finish(k + 1, acc, total)
        return 0

    lax.fori_loop(0, SECTIONS - 1, forward, 0)

    acc = jnp.zeros((ROWS, R), jnp.float32)
    for c in range(E // STEP):
        at = slice(c * STEP, (c + 1) * STEP)
        rows = target[:, at]
        grad[:, at] = rows
        acc += nt_dot(rows, out_part(SECTIONS - 1, c))
    hid[...] = acc

    def backward(i, _):
        k = SECTIONS - 1 - i
        p = pre[k]
        inv = root[k]
        squash = jax.nn.sigmoid(p)
        act = hid[...] * squash * (1.0 + p * (1.0 - squash))
        inner = jnp.sum(act * p, axis=1, keepdims=True) * (1.0 / E)
        scaled = (inv * act).astype(jnp.bfloat16)
        back = inv * inv * inner
        wide = jnp.concatenate([back, back], axis=1)

        @pl.when(k == place[0])
        def _():
            hidden = (p * squash).astype(jnp.bfloat16)
            for c in range(E // STEP):
                at = slice(c * STEP, (c + 1) * STEP)
                part = tn_dot(hidden, grad[:, at]).astype(jnp.bfloat16)
                staged[2 * c] = part[:, :LANES]
                staged[2 * c + 1] = part[:, LANES:]
                part = tn_dot(kept[k, :, at], scaled).astype(jnp.bfloat16)
                grad_in[c * STEP // 8 : (c + 1) * STEP // 8] = part.reshape(STEP // 8, 8, R)

        @pl.when(k > 0)
        def _():
            acc = jnp.zeros((ROWS, R), jnp.float32)
            for c in range(E // STEP):
                at = slice(c * STEP, (c + 1) * STEP)
                rows = grad[:, at].astype(jnp.float32) + nt_dot(scaled, w_in[k, at])
                rows = (rows - wide * kept[k, :, at].astype(jnp.float32)).astype(jnp.bfloat16)
                grad[:, at] = rows
                acc += nt_dot(rows, out_part(k - 1, c))
            hid[...] = acc

        return 0

    lax.fori_loop(0, SECTIONS, backward, 0)
    for swapped in range(2):
        into_in, into_out = (kept_out, sent_out) if swapped == 0 else (sent_out, kept_out)

        @pl.when(core == swapped)
        def _():
            stores = []
            for z in range(RINGS):
                at = (z % 4, z // 4)
                stores.append(
                    pltpu.make_async_copy(
                        grad_in.at[pl.ds(z * COLS, COLS)], into_in.at[at], out_sems.at[0, z]
                    )
                )
                stores.append(
                    pltpu.make_async_copy(
                        staged.at[:, pl.ds(z * 8, 8), :], into_out.at[at], out_sems.at[1, z]
                    )
                )
            for c in stores:
                c.start()
            for c in stores:
                c.wait()


def run_chain(place, stream, target, parts_of):
    whole = pl.BlockSpec(memory_space=pltpu.VMEM)
    anywhere = pl.BlockSpec(memory_space=pl.ANY)
    parts = []
    for part in parts_of:
        blocks, rings = part.shape[:2]
        parts += [part.reshape(blocks, rings * 2 * TILE_ROWS, R), part]
    piece = jax.ShapeDtypeStruct((4, 4, COLS, 8, LANES), jnp.bfloat16)
    return pl.pallas_call(
        chain,
        out_shape=(piece, piece),
        in_specs=[pl.BlockSpec(memory_space=pltpu.SMEM), whole, whole] + len(parts) * [anywhere],
        out_specs=(anywhere, anywhere),
        scratch_shapes=[
            pltpu.VMEM((SECTIONS, E, R), jnp.bfloat16),
            pltpu.VMEM((SECTIONS, COLS, R, LANES), jnp.bfloat16),
            pltpu.VMEM((SECTIONS, ROWS, E), jnp.bfloat16),
            pltpu.VMEM((ROWS, E), jnp.bfloat16),
            pltpu.VMEM((SECTIONS, ROWS, R), jnp.float32),
            pltpu.VMEM((SECTIONS, ROWS, LANES), jnp.float32),
            pltpu.VMEM((ROWS, R), jnp.float32),
            pltpu.VMEM((E // 8, 8, R), jnp.bfloat16),
            pltpu.VMEM((COLS, R, LANES), jnp.bfloat16),
            pltpu.SemaphoreType.DMA((SECTIONS, 2 + RINGS)),
            pltpu.SemaphoreType.DMA((2, RINGS)),
        ],
        compiler_params=pltpu.CompilerParams(vmem_limit_bytes=60 * 1024 * 1024),
    )(place, stream, target, *parts)


def shifted(x, along, across):
    pairs = []
    for i in range(4):
        for j in range(4):
            for core, (di, dj) in enumerate(((along, across), (across, along))):
                target = 4 * ((i + di) % 4) + (j + dj) % 4
                pairs.append((2 * (4 * i + j) + core, 2 * target + core))
    return lax.ppermute(x, PLANE, pairs)


def swap_cores(x):
    return lax.ppermute(x, "dp_1", [(0, 1), (1, 0)])


def update(weight, grad, moment, variance, factor):
    scaled = factor * grad
    moment = BETA_ONE * moment + (1.0 - BETA_ONE) * scaled
    variance = BETA_TWO * variance + (1.0 - BETA_TWO) * scaled * scaled
    weight = weight.astype(jnp.float32) - STEP_RATE * moment / (jnp.sqrt(variance) + ADAM_EPS)
    return (weight[None], moment[None], variance[None])


def shards(
    stream_in,
    cotangent,
    norm_gain,
    weight_in,
    weight_out,
    moment_in,
    variance_in,
    moment_out,
    variance_out,
):
    section = lax.axis_index(SECTION)
    ring = lax.axis_index(RING)
    core = lax.axis_index("dp_1")
    first = core == 0
    dp = lax.axis_index(DP)
    in_slice = weight_in[0]
    out_slice = weight_out[0]
    own_rows = in_slice.shape[0]
    gain = lax.dynamic_slice_in_dim(norm_gain[0], dp * own_rows, own_rows).astype(jnp.float32)

    in_part = (in_slice.astype(jnp.float32) * gain[:, None]).astype(jnp.bfloat16)
    in_part = in_part.reshape(COLS, 4, LANES)
    out_part = out_slice.reshape(4, COLS, LANES).transpose(1, 0, 2)
    other = swap_cores(jnp.where(first, out_part, in_part))
    of_in = jnp.concatenate([in_part, other], axis=0).reshape(COLS, 8, LANES)
    of_out = jnp.concatenate([other, out_part], axis=1)
    pair = jnp.where(first, of_in, of_out)
    column = lax.all_gather(pair[None], RING, axis=0, tiled=True)
    shared = lax.all_gather(column[:SHARED][None], PLANE, axis=0, tiled=True)
    block = column[SHARED:][None]
    row = lax.optimization_barrier(
        jnp.concatenate([block] + [shifted(block, by, 0) for by in (1, -1, 2)], axis=0)
    )
    up, down = shifted(row, 0, 1), shifted(row, 0, -1)
    half = row.shape[1] // 2
    beyond = jnp.concatenate([shifted(up[:, :half], 0, 1), shifted(down[:, half:], 0, -1)], axis=1)
    own = [row, up, down, beyond]
    sibling = [swap_cores(part) for part in own]

    place = jnp.stack([section, core]).astype(jnp.int32)
    kept, sent = run_chain(
        place, stream_in.reshape(ROWS, E), cotangent.reshape(ROWS, E), [shared] + own + sibling
    )
    total = kept.astype(jnp.float32) + swap_cores(sent).astype(jnp.float32)
    for axis in ("ring_1", "ring_0"):
        pieces = lax.all_to_all(total.astype(jnp.bfloat16), axis, 0, 0, tiled=True)
        total = jnp.sum(pieces.astype(jnp.float32), axis=0)
    chip_gain = lax.dynamic_slice_in_dim(norm_gain[0], ring * 2 * own_rows, 2 * own_rows)
    total = total.reshape(2 * own_rows, LANES)
    total = total * jnp.where(first, chip_gain.astype(jnp.float32), 1.0)[:, None]
    chip_sum = jnp.sum(total * total)
    device_count = lax.axis_size(EVERY)
    sums = jnp.broadcast_to(chip_sum, (device_count, 1, LANES))
    sums = lax.all_to_all(sums, EVERY, 0, 0, tiled=True)
    norm_total = jnp.sum(sums[:, 0, 0])

    as_in = total.reshape(2, own_rows, LANES)
    as_out = total.reshape(COLS, 2, 4, LANES)
    mine = jnp.where(first, as_in[0], as_out[:, 1].reshape(own_rows, LANES))
    theirs = jnp.where(first, as_in[1], as_out[:, 0].reshape(own_rows, LANES))
    arrived = swap_cores(theirs)
    grad_w_in = jnp.where(first, mine, arrived)
    grad_w_out = jnp.where(first, arrived, mine).reshape(COLS, 4, LANES)
    grad_w_out = grad_w_out.transpose(1, 0, 2).reshape(4, E)

    count_all = 2.0 * E * R * SECTIONS
    factor = jnp.minimum(1.0, lax.rsqrt(norm_total / count_all + CLIP_EPS))
    new_in, new_moment_in, new_variance_in = update(
        in_slice, grad_w_in, moment_in[0], variance_in[0], factor
    )
    new_out, new_moment_out, new_variance_out = update(
        out_slice, grad_w_out, moment_out[0], variance_out[0], factor
    )
    return (new_in, new_moment_in, new_variance_in, new_out, new_moment_out, new_variance_out)


def solution(mesh):
    finer = Mesh(mesh.devices.reshape(4, 4, 4, 4, 2), EVERY)
    placed = (P(None, DP, None), P(None, DP, None), P(SECTION, None)) + 6 * (
        P(SECTION, DP, None),
    )
    return jax.shard_map(
        shards, mesh=finer, in_specs=placed, out_specs=6 * (P(SECTION, DP, None),), check_vma=False
    )
```
